32 devices in a mesh: seq: 8 (over y, x, core), batch: 4 (over z).
Axes of the slice: x: 2, y: 2, z: 4, core: 2. Of those that a mesh axis runs over, the one named last changes fastest.
Arguments:
- tokens: bfloat16 [4, 4096, 2048], P('batch', 'seq'), may hold values from -6 to 6
- w_qkv: bfloat16 [2048, 3072], replicated, may hold values from -0.125 to 0.125
- cotangent: bfloat16 [4, 4096, 1024], P('batch', 'seq'), may hold values from -6 to 6
Outputs:
- attended: bfloat16 [4, 4096, 1024], P('batch', 'seq')
- token_grad: bfloat16 [4, 4096, 2048], P('batch', 'seq')
- weight_grad: float32 [2048, 3072], P('seq')
The draws below stay inside these ranges and needn't reach their ends.
All inputs are finite; a program needn't handle non-finite values.
Results may differ from the reference program's by a relative error of at most 0.0064.
Values sent between devices are 32-bit elements; how exact they have to be, the bound alone decides.
A program may use at most 192 MiB of HBM per device.

```python
import jax
import jax.numpy as jnp
from jax import lax

D = 2048
HEADS = 8
DH = 128
BLK = 512
HD = 1024
SEQS = 4
LENGTH = 4096


def block_scale(rng, dims, pieces, low, high):
    level, own = 1.0, jax.random.fold_in(rng, 6)
    for dim, blocks in pieces:
        draws = jnp.exp(jax.random.uniform(jax.random.fold_in(own, dim), (blocks,), jnp.float32, low / len(pieces), high / len(pieces)))
        level = level * jnp.repeat(draws, dims[dim] // blocks).reshape([-1 if axis == dim else 1 for axis in range(len(dims))])
    return level


def bell_draw(rng, shape, spread, reach, split=(), dtype=jnp.bfloat16):
    array = spread * jax.random.normal(rng, shape, jnp.float32)
    if split:
        array = array * block_scale(rng, shape, split, -0.22, 0.18)
    return jnp.clip(array, -reach, reach).astype(dtype)


def setup_inputs(seed: int = 0) -> dict:
    keys = jax.random.split(jax.random.key(seed), 4)
    tokens = bell_draw(keys[0], (SEQS, LENGTH, D), 1.0, 6.0, ((0, 4), (1, 8)))
    w_qkv = bell_draw(keys[1], (D, 3 * HD), D ** -0.5, 0.125)
    cotangent = bell_draw(keys[2], (SEQS, LENGTH, HD), 1.0, 6.0, ((0, 4), (1, 8)))
    return dict(tokens=tokens, w_qkv=w_qkv, cotangent=cotangent)


PRECISE = lax.Precision.HIGHEST

def exclusive_running(block_states, reverse):
    zero_block = jnp.zeros_like(block_states[:1])
    if reverse:
        totals = jnp.cumsum(block_states[::-1], axis=0)[::-1]
        return jnp.concatenate([totals[1:], zero_block], 0)
    totals = jnp.cumsum(block_states, axis=0)
    return jnp.concatenate([zero_block, totals[:-1]], 0)

def rounded(value):
    low = lax.optimization_barrier(value.astype(jnp.bfloat16))
    return low.astype(jnp.float32)

def one_sequence(seq_tokens, w_qkv, seq_cotangent):
    length = seq_tokens.shape[0]
    width = w_qkv.shape[1] // 3
    block_count = length // BLK
    projected = jnp.dot(seq_tokens, w_qkv, preferred_element_type=jnp.float32).astype(jnp.bfloat16)

    def to_heads(block):
        return block.reshape(block_count, BLK, HEADS, DH).astype(jnp.float32)
    queries = to_heads(projected[:, :width])
    key_heads = to_heads(projected[:, width:2 * width])
    value_heads = to_heads(projected[:, 2 * width:])
    position = jnp.arange(length).astype(jnp.float32)
    pos_scale = DH ** (-0.5) / jnp.sqrt(position + 1.0)
    scaled_grad = (seq_cotangent.astype(jnp.float32) * pos_scale[:, None]).astype(jnp.bfloat16)
    grad_heads = to_heads(scaled_grad)
    kv_blocks = jnp.einsum('nrha,nrhb->nhab', key_heads, value_heads, precision=PRECISE)
    grad_blocks = jnp.einsum('nrha,nrhb->nhab', queries, grad_heads, precision=PRECISE)
    kv_before = exclusive_running(kv_blocks, False)
    grad_after = exclusive_running(grad_blocks, True)
    causal = jnp.arange(BLK)[:, None] >= jnp.arange(BLK)[None, :]
    scale_blocks = pos_scale.reshape(block_count, BLK)

    def one_block(block_items):
        query, key_part, value_part, grad_part, kv_state, grad_state, scale_part = block_items
        scores = rounded(jnp.where(causal, jnp.einsum('ihd,jhd->hij', query, key_part, precision=PRECISE), 0.0))
        grad_scores = rounded(jnp.where(causal, jnp.einsum('ihd,jhd->hij', grad_part, value_part, precision=PRECISE), 0.0))
        attended = jnp.einsum('hij,jhd->ihd', scores, value_part, precision=PRECISE)
        attended = (attended + jnp.einsum('ihd,hde->ihe', query, kv_state, precision=PRECISE)) * scale_part[:, None, None]
        query_grad = jnp.einsum('hij,jhd->ihd', grad_scores, key_part, precision=PRECISE)
        query_grad = query_grad + jnp.einsum('ihe,hde->ihd', grad_part, kv_state, precision=PRECISE)
        key_grad = jnp.einsum('hij,ihd->jhd', grad_scores, query, precision=PRECISE)
        key_grad = key_grad + jnp.einsum('jhe,hde->jhd', value_part, grad_state, precision=PRECISE)
        value_grad = jnp.einsum('hij,ihe->jhe', scores, grad_part, precision=PRECISE)
        value_grad = value_grad + jnp.einsum('jhd,hde->jhe', key_part, grad_state, precision=PRECISE)
        return (attended.astype(jnp.bfloat16), query_grad.astype(jnp.bfloat16), key_grad.astype(jnp.bfloat16), value_grad.astype(jnp.bfloat16))
    results = lax.map(one_block, (queries, key_heads, value_heads, grad_heads, kv_before, grad_after, scale_blocks))
    attended = results[0].reshape(length, width)
    qkv_grad = jnp.concatenate([results[1].reshape(length, width), results[2].reshape(length, width), results[3].reshape(length, width)], 1)
    token_grad = jnp.dot(qkv_grad, w_qkv.T, preferred_element_type=jnp.float32).astype(jnp.bfloat16)
    weight_part = jnp.dot(seq_tokens.T, qkv_grad, preferred_element_type=jnp.float32)
    return (attended, token_grad, weight_part)

def reference(tokens, w_qkv, cotangent):
    seq_total = tokens.shape[0]
    length = tokens.shape[1]
    attended_list = []
    token_list = []
    weight_sum = jnp.zeros(w_qkv.shape, jnp.float32)
    for number in range(seq_total):
        attended, token_grad, weight_part = one_sequence(tokens[number], w_qkv, cotangent[number])
        attended_list.append(attended)
        token_list.append(token_grad)
        weight_sum = weight_sum + weight_part
    weight_grad = weight_sum / jnp.sqrt(jnp.float32(seq_total * length))
    return (jnp.stack(attended_list, 0), jnp.stack(token_list, 0), weight_grad)
```

```python
import functools
import types

import jax
import jax.numpy as jnp
from jax import lax
from jax.experimental import pallas as pl
from jax.experimental.pallas import tpu as pltpu
from jax.sharding import PartitionSpec as P

HEADS = 8
DH = 128
BLK = 512
COLS = 128
PAIR = 2 * COLS
TILE = 256
MESH = pl.DeviceIdType.MESH
CROSS = ()


def bits_of(count):
    bits = count.bit_length() - 1
    assert count == 1 << bits
    return bits


def dot(left, right, left_dim, right_dim):
    return lax.dot_general(
        left, right, (((left_dim,), (right_dim,)), ((), ())), preferred_element_type=jnp.float32
    )


def wide(left, state, state_dim):
    high = state.astype(jnp.bfloat16)
    rest = (state - high.astype(jnp.float32)).astype(jnp.bfloat16)
    return dot(left, high, 1, state_dim) + dot(left, rest, 1, state_dim)


def lanes(start, size):
    return pl.ds(pl.multiple_of(start, COLS), size)


def step_kernel(seq_count, batch_count, grad_scale, names, x_hbm, w_hbm, c_hbm, a_hbm, t_hbm, o_hbm, *scratch):
    m = types.SimpleNamespace(**dict(zip(names, scratch)))
    bits = bits_of(seq_count) - 1
    chips = 1 << bits
    rows, width = x_hbm.shape
    head_width = c_hbm.shape[1]
    groups = head_width // PAIR
    pairs = 3 * groups
    chunks = 2 * pairs
    half = width // 2
    own_rows = width // seq_count
    rank = lax.axis_index("seq")
    core = rank % 2
    chip = rank // 2
    plane = lax.axis_index("batch")
    middle = batch_count // 2
    low_side = plane < middle
    depth = jnp.where(low_side, middle - 1 - plane, plane - middle)
    has_outer = jnp.where(low_side, plane > 0, plane < batch_count - 1)
    is_inner = depth == 0
    inner = jnp.where(low_side, plane + 1, plane - 1)
    outer = jnp.where(low_side, plane - 1, plane + 1)
    mate_id = {"seq": rank ^ 1}

    base = list(range(bits))
    turned = base[bits // 2 :] + base[: bits // 2]
    crossed = set(CROSS) if batch_count == 4 else set()
    ways = []
    for chunk in range(chunks):
        way = base if chunk % 2 == 0 else turned
        ways.append((["z"] if chunk // 2 in crossed else []) + way)
    cross_index = {chunk: i for i, chunk in enumerate(c for c in range(chunks) if c // 2 in crossed)}

    def local(source, target, sem):
        return pltpu.make_async_copy(source, target, sem)

    def remote(source, target, send, recv, device):
        return pltpu.make_async_remote_copy(
            src_ref=source, dst_ref=target, send_sem=send, recv_sem=recv, device_id=device, device_id_type=MESH
        )

    def w_part(group, part):
        column = lanes(part * head_width + group * PAIR, PAIR)
        return local(w_hbm.at[:, column], m.w_parts.at[part], m.w_sem.at[part])

    def w_tile(index):
        row = pl.ds(pl.multiple_of(index * TILE, TILE), TILE)
        return local(w_hbm.at[row], m.w_tiles.at[index % 2], m.t_sem.at[index % 2])

    def t_out(index):
        return local(m.t_tile.at[index % 2], t_hbm.at[:, lanes(index * TILE, TILE)], m.t_sem.at[2 + index % 2])

    def a_out(group):
        column = pl.ds(group * PAIR, PAIR)
        return local(m.grads.at[:, column], a_hbm.at[:, column], m.a_sem.at[group])

    def o_out(chunk):
        pair, side = chunk // 2, chunk % 2
        column = (pair % 3) * head_width + (pair // 3) * PAIR + side * COLS
        return local(m.from_inner.at[chunk], o_hbm.at[:, pl.ds(column, COLS)], m.o_sem.at[chunk])

    x_in = local(x_hbm, m.x_all, m.x_sem.at[0])
    c_in = local(c_hbm, m.grads, m.x_sem.at[1])
    for part in range(3):
        w_part(0, part).start()
        if part == 0:
            x_in.start()
    c_in.start()
    barrier = pltpu.get_barrier_semaphore()
    pl.semaphore_signal(barrier, inc=1, device_id=mate_id, device_id_type=MESH)
    for bit in range(bits):
        pl.semaphore_signal(barrier, inc=1, device_id={"seq": rank ^ (2 << bit)}, device_id_type=MESH)
    pl.semaphore_signal(barrier, inc=1, device_id={"batch": inner}, device_id_type=MESH)

    @pl.when(has_outer)
    def _():
        pl.semaphore_signal(barrier, inc=1, device_id={"batch": outer}, device_id_type=MESH)

    position = rank * rows + lax.broadcasted_iota(jnp.int32, (rows, COLS), 0)
    m.scale[...] = DH ** (-0.5) / jnp.sqrt(position.astype(jnp.float32) + 1.0)

    def project(group):
        @pl.loop(0, 3)
        def _(part):
            w_part(group, part).wait()
            m.qkv[:, lanes(part * head_width + group * PAIR, PAIR)] = dot(
                m.x_all[...], m.w_parts[part], 1, 0
            ).astype(m.qkv.dtype)
            if group + 1 < groups:
                w_part(group + 1, part).start()

    def head_columns(group, head):
        start = group * PAIR + head * DH
        return [lanes(part * head_width + start, DH) for part in range(3)] + [lanes(start, DH)]

    def first_swap(group):
        return remote(
            m.states.at[group, 1 - core], m.mates.at[group], m.swap_send.at[0, group], m.swap_recv.at[0, group], mate_id
        )

    def last_swap(group):
        return remote(
            m.gives.at[group], m.carry.at[group, core], m.swap_send.at[1, group], m.swap_recv.at[1, group], mate_id
        )

    def bit_swap(group, bit):
        return remote(
            m.totals.at[bit, group],
            m.others.at[bit, group],
            m.bit_send.at[bit, group],
            m.bit_recv.at[bit, group],
            {"seq": rank ^ (2 << bit)},
        )

    def takes(bit):
        return ((chip // (1 << bit)) % 2) != core

    def make_states(group):
        @pl.loop(0, 2)
        def _(head):
            q_at, k_at, v_at, g_at = head_columns(group, head)
            grad = (m.grads[:, g_at].astype(jnp.float32) * m.scale[...]).astype(jnp.bfloat16)
            m.grads[:, g_at] = grad
            m.states[group, 0, head] = dot(m.qkv[:, k_at], m.qkv[:, v_at], 0, 0)
            m.states[group, 1, head] = dot(m.qkv[:, q_at], grad, 0, 0)

        first_swap(group).start()

    def start_bit(group, bit):
        if bit == bits - 1:
            pl.when(jnp.logical_not(takes(bit)))(bit_swap(group, bit).start)
        else:
            bit_swap(group, bit).start()

    def chain_first(group):
        first_swap(group).wait_recv()
        m.totals[0, group] = m.states[group, core] + m.mates[group]
        start_bit(group, 0)
        m.carry[group, core] = jnp.zeros(m.mates.shape[1:], jnp.float32)

    def chain_bit(group, bit):
        last = bit == bits - 1
        if not last:
            bit_swap(group, bit).wait_recv()
            m.totals[bit + 1, group] = m.totals[bit, group] + m.others[bit, group]
            start_bit(group, bit + 1)

        @pl.when(takes(bit))
        def _():
            if last:
                bit_swap(group, bit).wait_recv()
            m.carry[group, core] += m.others[bit, group]

        if last:
            m.gives[group] = m.carry[group, core] + m.states[group, core]
            last_swap(group).start()

    chains = [
        [functools.partial(chain_first, group)] + [functools.partial(chain_bit, group, bit) for bit in range(bits)]
        for group in range(groups)
    ]

    def chain(group, count=None):
        count = len(chains[group]) if count is None else count
        for _ in range(min(count, len(chains[group]))):
            chains[group].pop(0)()

    def in_block(group):
        low = slice(0, TILE)
        high = slice(TILE, BLK)
        row = lax.broadcasted_iota(jnp.int32, (TILE, TILE), 0)
        col = lax.broadcasted_iota(jnp.int32, (TILE, TILE), 1)
        causal = row >= col

        @pl.loop(0, 2)
        def _(head):
            q_at, k_at, v_at, g_at = head_columns(group, head)
            out_at = lanes(head * DH, DH)

            def products(left_ref, left_at, right_at):
                def one(i, j, masked):
                    value = dot(left_ref[i, left_at], m.qkv[j, right_at], 1, 1)
                    if masked:
                        value = jnp.where(causal, value, 0.0)
                    return value.astype(jnp.bfloat16)

                m.tri[0] = one(low, low, True)
                m.tri[1] = one(high, low, False)
                m.tri[2] = one(high, high, True)

            def by_rows(index, ref, at):
                m.parts[index, low, out_at] = dot(m.tri[0], ref[low, at], 1, 0)
                m.parts[index, high, out_at] = dot(m.tri[1], ref[low, at], 1, 0) + dot(m.tri[2], ref[high, at], 1, 0)

            def by_columns(index, ref, at):
                m.parts[index, low, out_at] = dot(m.tri[0], ref[low, at], 0, 0) + dot(m.tri[1], ref[high, at], 0, 0)
                m.parts[index, high, out_at] = dot(m.tri[2], ref[high, at], 0, 0)

            products(m.qkv, q_at, k_at)
            by_rows(0, m.qkv, v_at)
            by_columns(3, m.grads, g_at)
            products(m.grads, g_at, v_at)
            by_rows(1, m.qkv, k_at)
            by_columns(2, m.qkv, q_at)

    def grad_swap(group, part):
        slot = group % 2
        return remote(
            m.g_send.at[slot, part],
            m.g_land.at[slot, part],
            m.g_ssem.at[group, part],
            m.g_rsem.at[group, part],
            mate_id,
        )

    def finish(group):
        slot = group % 2
        last_swap(group).wait_recv()
        if group >= 2:
            for part in range(3):
                grad_swap(group - 2, part).wait_send()

        @pl.loop(0, 2)
        def _(head):
            q_at, k_at, v_at, g_at = head_columns(group, head)
            out_at = lanes(head * DH, DH)
            query, key, value, grad = m.qkv[:, q_at], m.qkv[:, k_at], m.qkv[:, v_at], m.grads[:, g_at]
            kv, gs = m.carry[group, 0, head], m.carry[group, 1, head]
            attended = (m.parts[0, :, out_at] + wide(query, kv, 0)) * m.scale[...]
            results = (
                m.parts[1, :, out_at] + wide(grad, kv, 1),
                m.parts[2, :, out_at] + wide(value, gs, 1),
                m.parts[3, :, out_at] + wide(key, gs, 0),
            )
            m.grads[:, g_at] = attended.astype(jnp.bfloat16)
            for part, at in enumerate((q_at, k_at, v_at)):
                low = results[part].astype(jnp.bfloat16)
                m.qkv[:, at] = low
                m.g_cat[part, 0:rows, out_at] = low
                m.g_send[slot, part, head] = low.astype(jnp.float32)

        for part in range(3):
            grad_swap(group, part).start()
        a_out(group).start()

    spare = rows // COLS
    x_swap = remote(
        m.mine.at[pl.ds(chunks - spare, spare)],
        m.mine.at[pl.ds(chunks - 2 * spare, spare)],
        m.x_sem.at[2],
        m.x_sem.at[3],
        mate_id,
    )

    def turn_tokens():
        @pl.loop(0, chips)
        def _(index):
            owner = chip ^ index
            m.turned[...] = m.x_all[:, lanes(owner * 2 * own_rows, 2 * own_rows)].T
            row = pl.ds(pl.multiple_of(index * own_rows, own_rows), own_rows)
            m.x_cat[row, 0:rows] = m.turned[pl.ds(pl.multiple_of(core * own_rows, own_rows), own_rows), :]
            other = m.turned[pl.ds(pl.multiple_of((1 - core) * own_rows, own_rows), own_rows), :]
            for piece in range(spare):
                m.mine[chunks - spare + piece, row, :] = other[:, piece * COLS : (piece + 1) * COLS].astype(jnp.float32)

        x_swap.start()

    def join_tokens():
        x_swap.wait_recv()
        for piece in range(spare):
            at = rows + piece * COLS
            m.x_cat[:, at : at + COLS] = m.mine[chunks - 2 * spare + piece].astype(jnp.bfloat16)

    keeps_low = jnp.where(is_inner, 0, 1)

    def multiply(pair):
        group, part = pair // 3, pair % 3
        grad_swap(group, part).wait_recv()
        for side in range(2):
            m.g_cat[part, rows : 2 * rows, side * COLS : (side + 1) * COLS] = m.g_land[group % 2, part, side].astype(
                jnp.bfloat16
            )
        if group == groups - 1 and part == 0:
            x_swap.wait_send()

        @pl.loop(0, chips)
        def _(index):
            value = dot(
                m.x_cat[pl.ds(pl.multiple_of(index * own_rows, own_rows), own_rows), :], m.g_cat[part], 1, 0
            )
            for side in range(2):
                chunk = 2 * pair + side
                way = [bit for bit in ways[chunk] if bit != "z"]
                spot = sum((index // (1 << bit) % 2) * (1 << (bits - 1 - k)) for k, bit in enumerate(way))
                piece = value[:, side * COLS : (side + 1) * COLS]
                if chunk in cross_index:
                    part_rows = own_rows // 2
                    for low in range(2):
                        far = keeps_low if low else 1 - keeps_low
                        row = pl.multiple_of((far * chips + spot) * part_rows, part_rows)
                        m.mine[chunk, pl.ds(row, part_rows), :] = piece[low * part_rows : (low + 1) * part_rows]
                else:
                    row = pl.multiple_of(spot * own_rows, own_rows)
                    m.mine[chunk, pl.ds(row, own_rows), :] = piece

    def step_copy(chunk, step):
        size = half >> (step + 1)
        way = ways[chunk][step]
        land = m.lands[step].at[cross_index[chunk] if step == bits else chunk]
        device = {"batch": plane ^ 1} if way == "z" else {"seq": rank ^ (2 << way)}
        return remote(
            m.mine.at[chunk, pl.ds(size, size)], land, m.step_send.at[step, chunk], m.step_recv.at[step, chunk], device
        )

    def kept_rows(chunk):
        return own_rows // 2 if chunk in cross_index else own_rows

    def inward(chunk, to_inner):
        if to_inner:
            target = m.from_inner.at[chunk]
        else:
            target = m.from_outer.at[chunk, pl.ds(0, kept_rows(chunk))]
        return target

    def inward_copy(chunk, leaf, to_inner):
        source = m.mine.at[chunk, pl.ds(0, kept_rows(chunk))] if leaf else m.from_outer.at[chunk]
        return remote(
            source,
            inward(chunk, to_inner),
            m.z_send.at[0, chunk],
            m.z_recv.at[1 if to_inner else 0, chunk],
            {"batch": inner},
        )

    def outward(chunk):
        return remote(
            m.from_inner.at[chunk], m.from_inner.at[chunk], m.z_send.at[1, chunk], m.z_recv.at[1, chunk], {"batch": outer}
        )

    lone = batch_count == 2

    def leave(chunk):
        @pl.when(jnp.logical_not(has_outer))
        def _():
            inward_copy(chunk, True, lone).start()

    def halve(chunk, step):
        step_copy(chunk, step).wait_recv()
        size = half >> (step + 1)
        land = m.lands[step].at[cross_index[chunk] if step == bits else chunk]
        if step + 1 < len(ways[chunk]):
            part = size // 2
            m.mine[chunk, pl.ds(part, part), :] += land[pl.ds(part, part), :]
            step_copy(chunk, step + 1).start()
            m.mine[chunk, pl.ds(0, part), :] += land[pl.ds(0, part), :]
        else:
            m.mine[chunk, pl.ds(0, size), :] += land[...]
            leave(chunk)

    def gather(chunk):
        if lone:
            return

        @pl.when(has_outer)
        def _():
            inward_copy(chunk, True, False).wait_recv()
            kept = kept_rows(chunk)
            if chunk in cross_index:
                m.from_outer[chunk, pl.ds(kept, kept), :] = m.mine[chunk, pl.ds(0, kept), :]
            else:
                m.from_outer[chunk] += m.mine[chunk, pl.ds(0, kept), :]

        @pl.when(has_outer & is_inner)
        def _():
            inward_copy(chunk, False, True).start()

        if batch_count > 4:

            @pl.when(has_outer & jnp.logical_not(is_inner))
            def _():
                inward_copy(chunk, False, False).start()

    def close(chunk):
        inward_copy(chunk, lone, True).wait_recv()

        @pl.when(is_inner)
        def _():
            own = m.mine[chunk, pl.ds(0, own_rows), :] if lone else m.from_outer[chunk]
            m.from_inner[chunk] = (m.from_inner[chunk] + own) * grad_scale

        @pl.when(has_outer)
        def _():
            outward(chunk).start()

        o_out(chunk).start()

    tiles = width // TILE

    def token_tiles(first, count):
        @pl.loop(first, first + count)
        def _(index):
            w_tile(index).wait()

            @pl.when(index >= 2)
            def _():
                t_out(index - 2).wait()

            m.t_tile[index % 2] = dot(m.qkv[...], m.w_tiles[index % 2], 1, 1).astype(m.t_tile.dtype)
            t_out(index).start()

            @pl.when(index + 2 < tiles)
            def _():
                w_tile(index + 2).start()

    def open_pair(pair):
        for chunk in (2 * pair, 2 * pair + 1):
            step_copy(chunk, 0).start()

    events = {}
    for pair in range(pairs):
        for chunk in (2 * pair, 2 * pair + 1):
            count = len(ways[chunk])
            for step in range(count):
                events.setdefault(pair + step, []).append((-step, chunk, functools.partial(halve, chunk, step)))
            events.setdefault(pair + count, []).append((-count, chunk, functools.partial(gather, chunk)))
            events.setdefault(pair + count + 1, []).append((-count - 1, chunk, functools.partial(close, chunk)))

    def run_events(slot):
        for _, _, event in sorted(events.get(slot, []), key=lambda item: item[:2]):
            event()

    x_in.wait()
    project(0)
    c_in.wait()
    pl.semaphore_wait(barrier, bits + 2 + has_outer.astype(jnp.int32))
    make_states(0)
    turn_tokens()
    chain(0, 1)
    project(1)
    chain(0, 1)
    make_states(1)
    in_block(0)
    chain(0)
    chain(1, 1)
    join_tokens()
    finish(0)
    in_block(1)
    chain(1, 1)
    for pair in range(3):
        multiply(pair)
        if pair < 2:
            open_pair(pair)
    for index in range(2):
        w_tile(index).start()

    chain(1)
    finish(1)
    project(2)
    make_states(2)
    per_slot = {
        0: [lambda: multiply(3), lambda: chain(2, 1), lambda: multiply(4), lambda: project(3)],
        1: [lambda: multiply(5), lambda: make_states(3), lambda: chain(2, 1)],
        2: [lambda: in_block(2), lambda: chain(2), lambda: chain(3, 1)],
        3: [lambda: finish(2), lambda: in_block(3), lambda: multiply(6)],
        4: [lambda: multiply(7), lambda: chain(3, 1), lambda: multiply(8)],
        5: [lambda: chain(3), lambda: finish(3)],
        6: [lambda: multiply(9), lambda: multiply(10)],
        7: [lambda: multiply(11)],
    }
    for index in range(tiles // 2):
        per_slot.setdefault(8 + index, []).append(functools.partial(token_tiles, 2 * index, 2))
    for slot in range(max(max(events), max(per_slot)) + 1):
        run_events(slot)
        if slot + 2 < pairs:
            open_pair(slot + 2)
        for task in per_slot.get(slot, []):
            task()

    x_swap_pending = groups < 1
    assert not x_swap_pending
    for index in range(tiles - 2, tiles):
        t_out(index).wait()
    for group in range(groups):
        a_out(group).wait()
        first_swap(group).wait_send()
        last_swap(group).wait_send()
        for bit in range(bits):
            if bit == bits - 1:
                pl.when(jnp.logical_not(takes(bit)))(bit_swap(group, bit).wait_send)
            else:
                bit_swap(group, bit).wait_send()
        if group >= groups - 2:
            for part in range(3):
                grad_swap(group, part).wait_send()
    for chunk in range(chunks):
        for step in range(len(ways[chunk])):
            step_copy(chunk, step).wait_send()
        if lone:
            inward_copy(chunk, True, True).wait_send()
        else:

            @pl.when(jnp.logical_not(has_outer))
            def _():
                inward_copy(chunk, True, False).wait_send()

            @pl.when(has_outer)
            def _():
                inward_copy(chunk, False, True).wait_send()
                outward(chunk).wait_send()

        o_out(chunk).wait()


def body(tokens, w_qkv, cotangent):
    rows, width = tokens.shape[1:]
    columns = w_qkv.shape[1]
    head_width = columns // 3
    assert rows == BLK and head_width == HEADS * DH
    seq_count = lax.axis_size("seq")
    batch_count = lax.axis_size("batch")
    bits = bits_of(seq_count) - 1
    groups = head_width // PAIR
    chunks = columns // COLS
    half = width // 2
    own_rows = width // seq_count
    crossed = 2 * len(CROSS)
    grad_scale = float(batch_count * seq_count * rows) ** -0.5
    f32, bf16 = jnp.float32, jnp.bfloat16
    state = (2, DH, DH)
    sizes = dict(
        x_all=pltpu.VMEM((rows, width), bf16),
        x_cat=pltpu.VMEM((half, 2 * rows), bf16),
        turned=pltpu.VMEM((2 * own_rows, rows), bf16),
        w_parts=pltpu.VMEM((3, width, PAIR), bf16),
        w_tiles=pltpu.VMEM((2, TILE, columns), bf16),
        t_tile=pltpu.VMEM((2, rows, TILE), bf16),
        qkv=pltpu.VMEM((rows, columns), bf16),
        grads=pltpu.VMEM((rows, head_width), bf16),
        scale=pltpu.VMEM((rows, COLS), f32),
        parts=pltpu.VMEM((4, rows, PAIR), f32),
        tri=pltpu.VMEM((3, TILE, TILE), bf16),
        states=pltpu.VMEM((groups, 2) + state, f32),
        mates=pltpu.VMEM((groups,) + state, f32),
        gives=pltpu.VMEM((groups,) + state, f32),
        totals=pltpu.VMEM((bits, groups) + state, f32),
        others=pltpu.VMEM((bits, groups) + state, f32),
        carry=pltpu.VMEM((groups, 2) + state, f32),
        g_send=pltpu.VMEM((2, 3, 2, rows, COLS), f32),
        g_land=pltpu.VMEM((2, 3, 2, rows, COLS), f32),
        g_cat=pltpu.VMEM((3, 2 * rows, PAIR), bf16),
        mine=pltpu.VMEM((chunks, half, COLS), f32),
        lands=[pltpu.VMEM((chunks, half >> (step + 1), COLS), f32) for step in range(bits)]
        + [pltpu.VMEM((max(crossed, 1), half >> (bits + 1), COLS), f32)],
        from_outer=pltpu.VMEM((chunks, own_rows, COLS), f32),
        from_inner=pltpu.VMEM((chunks, own_rows, COLS), f32),
        w_sem=pltpu.SemaphoreType.DMA((3,)),
        x_sem=pltpu.SemaphoreType.DMA((4,)),
        t_sem=pltpu.SemaphoreType.DMA((4,)),
        a_sem=pltpu.SemaphoreType.DMA((groups,)),
        o_sem=pltpu.SemaphoreType.DMA((chunks,)),
        swap_send=pltpu.SemaphoreType.DMA((2, groups)),
        swap_recv=pltpu.SemaphoreType.DMA((2, groups)),
        bit_send=pltpu.SemaphoreType.DMA((bits, groups)),
        bit_recv=pltpu.SemaphoreType.DMA((bits, groups)),
        g_ssem=pltpu.SemaphoreType.DMA((groups, 3)),
        g_rsem=pltpu.SemaphoreType.DMA((groups, 3)),
        step_send=pltpu.SemaphoreType.DMA((bits + 1, chunks)),
        step_recv=pltpu.SemaphoreType.DMA((bits + 1, chunks)),
        z_send=pltpu.SemaphoreType.DMA((2, chunks)),
        z_recv=pltpu.SemaphoreType.DMA((2, chunks)),
    )
    attended, token_grad, weight_grad = pl.pallas_call(
        functools.partial(step_kernel, seq_count, batch_count, grad_scale, tuple(sizes)),
        out_shape=(
            jax.ShapeDtypeStruct((rows, head_width), bf16),
            jax.ShapeDtypeStruct((rows, width), bf16),
            jax.ShapeDtypeStruct((own_rows, columns), f32),
        ),
        in_specs=[pl.BlockSpec(memory_space=pl.ANY)] * 3,
        out_specs=[pl.BlockSpec(memory_space=pl.ANY)] * 3,
        scratch_shapes=list(sizes.values()),
        compiler_params=pltpu.CompilerParams(
            collective_id=0, has_side_effects=True, vmem_limit_bytes=62 * 1024 * 1024
        ),
    )(tokens[0], w_qkv, cotangent[0])
    return attended[None], token_grad[None], weight_grad


def solution(mesh):
    return jax.shard_map(
        body,
        mesh=mesh,
        in_specs=(P("batch", "seq", None), P(), P("batch", "seq", None)),
        out_specs=(P("batch", "seq", None), P("batch", "seq", None), P("seq", None)),
        check_vma=False,
    )
```

```python
import functools
import types

import jax
import jax.numpy as jnp
from jax import lax
from jax.experimental import pallas as pl
from jax.experimental.pallas import tpu as pltpu
from jax.sharding import PartitionSpec as P

HEADS = 8
DH = 128
BLK = 512
COLS = 128
PAIR = 2 * COLS
TILE = 256
MESH = pl.DeviceIdType.MESH
CROSS = (2, 5)
SEQUENCE = (0, 1, 3, 2, 4, 5, 6, 7, 8, 9, 10, 11)
PLACES = 6
SPLIT = {10: 2, 11: 2}
EARLY = 4
EARLY_LAGS = (1, 2, 3)
MID_LAGS = (0, 1, 2)
LAST_LAGS = (0, 2, 4)


def bits_of(count):
    bits = count.bit_length() - 1
    assert count == 1 << bits
    return bits


def dot(left, right, left_dim, right_dim):
    return lax.dot_general(
        left, right, (((left_dim,), (right_dim,)), ((), ())), preferred_element_type=jnp.float32
    )


def wide(left, state, state_dim):
    high = state.astype(jnp.bfloat16)
    rest = (state - high.astype(jnp.float32)).astype(jnp.bfloat16)
    return dot(left, high, 1, state_dim) + dot(left, rest, 1, state_dim)


def lanes(start, size):
    return pl.ds(pl.multiple_of(start, COLS), size)


def step_kernel(seq_count, batch_count, grad_scale, names, x_hbm, w_hbm, c_hbm, a_hbm, t_hbm, o_hbm, *scratch):
    m = types.SimpleNamespace(**dict(zip(names, scratch)))
    bits = bits_of(seq_count) - 1
    chips = 1 << bits
    rows, width = x_hbm.shape
    head_width = c_hbm.shape[1]
    groups = head_width // PAIR
    pairs = 3 * groups
    chunks = 2 * pairs
    half = width // 2
    own_rows = width // seq_count
    rank = lax.axis_index("seq")
    core = rank % 2
    chip = rank // 2
    plane = lax.axis_index("batch")
    middle = batch_count // 2
    low_side = plane < middle
    depth = jnp.where(low_side, middle - 1 - plane, plane - middle)
    has_outer = jnp.where(low_side, plane > 0, plane < batch_count - 1)
    is_inner = depth == 0
    inner = jnp.where(low_side, plane + 1, plane - 1)
    outer = jnp.where(low_side, plane - 1, plane + 1)
    mate_id = {"seq": rank ^ 1}

    base = list(range(bits))
    turned = base[bits // 2 :] + base[: bits // 2]
    ways = [base, turned]
    crossed = set(CROSS) if batch_count == 4 else set()
    assert sorted(SEQUENCE) == list(range(pairs))
    places = [(pair, sub) for pair in SEQUENCE for sub in range(SPLIT.get(pair, 1))]

    def units_of(position):
        pair, sub = places[position]
        count = SPLIT.get(pair, 1)
        return [
            types.SimpleNamespace(
                position=position,
                chunk=2 * pair + side,
                side=side,
                sub=sub,
                count=count,
                crossed=pair in crossed,
                place=(position % PLACES) * 2 + side,
                kept=own_rows // 2 if pair in crossed else own_rows // count,
                rows=pl.ds(sub * (own_rows // count), own_rows // count),
                first=sub * (own_rows // count),
            )
            for side in range(2)
        ]

    def earlier(unit):
        if unit.position < PLACES:
            return None
        return units_of(unit.position - PLACES)[unit.side]

    def local(source, target, sem):
        return pltpu.make_async_copy(source, target, sem)

    def remote(source, target, send, recv, device):
        return pltpu.make_async_remote_copy(
            src_ref=source, dst_ref=target, send_sem=send, recv_sem=recv, device_id=device, device_id_type=MESH
        )

    def w_part(group, part):
        column = lanes(part * head_width + group * PAIR, PAIR)
        return local(w_hbm.at[:, column], m.w_parts.at[part], m.w_sem.at[part])

    def w_tile(index):
        row = pl.ds(pl.multiple_of(index * TILE, TILE), TILE)
        return local(w_hbm.at[row], m.w_tiles.at[index % 2], m.t_sem.at[index % 2])

    def t_out(index):
        return local(m.t_tile.at[index % 2], t_hbm.at[:, lanes(index * TILE, TILE)], m.t_sem.at[2 + index % 2])

    def a_out(group):
        column = pl.ds(group * PAIR, PAIR)
        return local(m.grads.at[:, column], a_hbm.at[:, column], m.a_sem.at[group])

    def o_out(unit):
        group, spot = unit.chunk // 6, unit.chunk % 6
        column = (spot % 3) * head_width + group * PAIR + (spot // 3) * COLS
        row = unit.rows
        return local(m.from_inner.at[unit.chunk, row], o_hbm.at[row, pl.ds(column, COLS)], m.o_sem.at[unit.place])

    x_in = local(x_hbm, m.x_all, m.x_sem.at[0])
    c_in = local(c_hbm, m.grads, m.x_sem.at[1])
    for part in range(3):
        w_part(0, part).start()
        if part == 0:
            x_in.start()
    c_in.start()
    barrier = pltpu.get_barrier_semaphore()
    pl.semaphore_signal(barrier, inc=1, device_id=mate_id, device_id_type=MESH)
    for bit in range(bits):
        pl.semaphore_signal(barrier, inc=1, device_id={"seq": rank ^ (2 << bit)}, device_id_type=MESH)
    pl.semaphore_signal(barrier, inc=1, device_id={"batch": inner}, device_id_type=MESH)

    @pl.when(has_outer)
    def _():
        pl.semaphore_signal(barrier, inc=1, device_id={"batch": outer}, device_id_type=MESH)

    position = rank * rows + lax.broadcasted_iota(jnp.int32, (rows, COLS), 0)
    m.scale[...] = DH ** (-0.5) / jnp.sqrt(position.astype(jnp.float32) + 1.0)

    def project(group):
        @pl.loop(0, 3)
        def _(part):
            w_part(group, part).wait()
            m.qkv[:, lanes(part * head_width + group * PAIR, PAIR)] = dot(
                m.x_all[...], m.w_parts[part], 1, 0
            ).astype(m.qkv.dtype)
            if group + 1 < groups:
                w_part(group + 1, part).start()

    def head_columns(group, head):
        start = group * PAIR + head * DH
        return [lanes(part * head_width + start, DH) for part in range(3)] + [lanes(start, DH)]

    def first_swap(group):
        return remote(
            m.states.at[group, 1 - core], m.mates.at[group], m.swap_send.at[0, group], m.swap_recv.at[0, group], mate_id
        )

    def last_swap(group):
        return remote(
            m.gives.at[group], m.carry.at[group, core], m.swap_send.at[1, group], m.swap_recv.at[1, group], mate_id
        )

    def bit_swap(group, bit):
        return remote(
            m.totals.at[bit, group],
            m.others.at[bit, group],
            m.bit_send.at[bit, group],
            m.bit_recv.at[bit, group],
            {"seq": rank ^ (2 << bit)},
        )

    def takes(bit):
        return ((chip // (1 << bit)) % 2) != core

    def make_states(group):
        @pl.loop(0, 2)
        def _(head):
            q_at, k_at, v_at, g_at = head_columns(group, head)
            grad = (m.grads[:, g_at].astype(jnp.float32) * m.scale[...]).astype(jnp.bfloat16)
            m.grads[:, g_at] = grad
            m.states[group, 0, head] = dot(m.qkv[:, k_at], m.qkv[:, v_at], 0, 0)
            m.states[group, 1, head] = dot(m.qkv[:, q_at], grad, 0, 0)

        first_swap(group).start()

    def start_bit(group, bit):
        if bit == bits - 1:
            pl.when(jnp.logical_not(takes(bit)))(bit_swap(group, bit).start)
        else:
            bit_swap(group, bit).start()

    def chain_first(group):
        first_swap(group).wait_recv()
        m.totals[0, group] = m.states[group, core] + m.mates[group]
        start_bit(group, 0)
        m.carry[group, core] = jnp.zeros(m.mates.shape[1:], jnp.float32)

    def chain_bit(group, bit):
        last = bit == bits - 1
        if not last:
            bit_swap(group, bit).wait_recv()
            m.totals[bit + 1, group] = m.totals[bit, group] + m.others[bit, group]
            start_bit(group, bit + 1)

        @pl.when(takes(bit))
        def _():
            if last:
                bit_swap(group, bit).wait_recv()
            m.carry[group, core] += m.others[bit, group]

        if last:
            m.gives[group] = m.carry[group, core] + m.states[group, core]
            last_swap(group).start()

    chains = [
        [functools.partial(chain_first, group)] + [functools.partial(chain_bit, group, bit) for bit in range(bits)]
        for group in range(groups)
    ]

    def chain(group, count=None):
        count = len(chains[group]) if count is None else count
        for _ in range(min(count, len(chains[group]))):
            chains[group].pop(0)()

    def in_block(group, first=0, count=2):
        low = slice(0, TILE)
        high = slice(TILE, BLK)
        row = lax.broadcasted_iota(jnp.int32, (TILE, TILE), 0)
        col = lax.broadcasted_iota(jnp.int32, (TILE, TILE), 1)
        causal = row >= col

        @pl.loop(first, first + count)
        def _(head):
            q_at, k_at, v_at, g_at = head_columns(group, head)
            out_at = lanes(head * DH, DH)

            def products(left_ref, left_at, right_at):
                def one(i, j, masked):
                    value = dot(left_ref[i, left_at], m.qkv[j, right_at], 1, 1)
                    if masked:
                        value = jnp.where(causal, value, 0.0)
                    return value.astype(jnp.bfloat16)

                m.tri[0] = one(low, low, True)
                m.tri[1] = one(high, low, False)
                m.tri[2] = one(high, high, True)

            def by_rows(index, ref, at):
                m.parts[index, low, out_at] = dot(m.tri[0], ref[low, at], 1, 0)
                m.parts[index, high, out_at] = dot(m.tri[1], ref[low, at], 1, 0) + dot(m.tri[2], ref[high, at], 1, 0)

            def by_columns(index, ref, at):
                m.parts[index, low, out_at] = dot(m.tri[0], ref[low, at], 0, 0) + dot(m.tri[1], ref[high, at], 0, 0)
                m.parts[index, high, out_at] = dot(m.tri[2], ref[high, at], 0, 0)

            products(m.qkv, q_at, k_at)
            by_rows(0, m.qkv, v_at)
            by_columns(3, m.grads, g_at)
            products(m.grads, g_at, v_at)
            by_rows(1, m.qkv, k_at)
            by_columns(2, m.qkv, q_at)

    def grad_swap(group, spot):
        slot = group % 2
        return remote(
            m.g_send.at[slot, spot],
            m.g_land.at[slot, spot],
            m.g_ssem.at[slot, spot],
            m.g_rsem.at[slot, spot],
            mate_id,
        )

    def finish(group):
        slot = group % 2
        last_swap(group).wait_recv()

        @pl.loop(0, 2)
        def _(head):
            q_at, k_at, v_at, g_at = head_columns(group, head)
            out_at = lanes(head * DH, DH)
            query, key, value, grad = m.qkv[:, q_at], m.qkv[:, k_at], m.qkv[:, v_at], m.grads[:, g_at]
            kv, gs = m.carry[group, 0, head], m.carry[group, 1, head]

            def give(part, at, result):
                spot = 3 * head + part
                low = result.astype(jnp.bfloat16)
                m.qkv[:, at] = low
                m.g_cat[spot // 2, 0:rows, lanes(spot % 2 * COLS, COLS)] = low
                if group >= 2:
                    grad_swap(group - 2, spot).wait_send()
                m.g_send[slot, spot] = low.astype(jnp.float32)
                grad_swap(group, spot).start()

            give(0, q_at, m.parts[1, :, out_at] + wide(grad, kv, 1))
            give(1, k_at, m.parts[2, :, out_at] + wide(value, gs, 1))
            give(2, v_at, m.parts[3, :, out_at] + wide(key, gs, 0))
            attended = (m.parts[0, :, out_at] + wide(query, kv, 0)) * m.scale[...]
            m.grads[:, g_at] = attended.astype(jnp.bfloat16)

        a_out(group).start()

    spare = rows // COLS

    def x_swap(index):
        row = pl.ds(pl.multiple_of(index * own_rows, own_rows), own_rows)
        return remote(
            m.mine.at[pl.ds(chunks - spare, spare), row],
            m.mine.at[pl.ds(chunks - 2 * spare, spare), row],
            m.x_send.at[index],
            m.x_recv.at[index],
            mate_id,
        )

    def turn_tokens(first, last):
        @pl.loop(first, last)
        def _(index):
            owner = chip ^ index
            m.turned[...] = m.x_all[:, lanes(owner * 2 * own_rows, 2 * own_rows)].T
            row = pl.ds(pl.multiple_of(index * own_rows, own_rows), own_rows)
            m.x_cat[row, 0:rows] = m.turned[pl.ds(pl.multiple_of(core * own_rows, own_rows), own_rows), :]
            other = m.turned[pl.ds(pl.multiple_of((1 - core) * own_rows, own_rows), own_rows), :]
            for piece in range(spare):
                m.mine[chunks - spare + piece, row, :] = other[:, piece * COLS : (piece + 1) * COLS].astype(jnp.float32)
            x_swap(index).start()

    def join_tokens():
        @pl.loop(0, chips)
        def _(index):
            x_swap(index).wait_recv()
            row = pl.ds(pl.multiple_of(index * own_rows, own_rows), own_rows)
            for piece in range(spare):
                at = rows + piece * COLS
                m.x_cat[row, at : at + COLS] = m.mine[chunks - 2 * spare + piece, row, :].astype(jnp.bfloat16)

    keeps_low = jnp.where(is_inner, 0, 1)

    ready = set()

    def multiply(pair):
        group = pair // 3
        ready.add(pair)
        for side in range(2):
            spot = 2 * (pair % 3) + side
            grad_swap(group, spot).wait_recv()
            m.g_cat[spot // 2, rows : 2 * rows, side * COLS : (side + 1) * COLS] = m.g_land[group % 2, spot].astype(
                jnp.bfloat16
            )
        if pair == (chunks - spare) // 2:
            for index in range(chips):
                x_swap(index).wait_send()
        count = 2 if pair in crossed else SPLIT.get(pair, 1)

        @pl.loop(0, chips)
        def _(index):
            value = dot(
                m.x_cat[pl.ds(pl.multiple_of(index * own_rows, own_rows), own_rows), :], m.g_cat[pair % 3], 1, 0
            )
            for side, way in enumerate(ways):
                spot = sum((index // (1 << bit) % 2) * (1 << (bits - 1 - k)) for k, bit in enumerate(way))
                part_rows = own_rows // count
                for sub in range(count):
                    block = sub
                    if pair in crossed:
                        block = 1 - keeps_low if sub == 0 else keeps_low
                    row = pl.multiple_of((block * chips + spot) * part_rows, part_rows)
                    m.mine[2 * pair + side, pl.ds(row, part_rows), :] = value[
                        sub * part_rows : (sub + 1) * part_rows, side * COLS : (side + 1) * COLS
                    ]

        if pair in crossed:
            for unit in units_of(places.index((pair, 0))):
                cross_copy(unit).start()

    def cross_copy(unit):
        index = CROSS.index(unit.chunk // 2) * 2 + unit.side
        return remote(
            m.mine.at[unit.chunk, pl.ds(half // 2, half // 2)],
            m.cross_land.at[index],
            m.cross_send.at[index],
            m.cross_recv.at[index],
            {"batch": plane ^ 1},
        )

    def step_size(unit, step):
        whole = half // 2 if unit.crossed else half // unit.count
        return whole >> (step + 1), unit.sub * whole

    def landing(unit, step):
        size, _ = step_size(unit, step)
        return m.lands[step].at[unit.place, pl.ds(0, size)]

    def step_copy(unit, step):
        size, start = step_size(unit, step)
        return remote(
            m.mine.at[unit.chunk, pl.ds(start + size, size)],
            landing(unit, step),
            m.step_send.at[step, unit.place],
            m.step_recv.at[step, unit.place],
            {"seq": rank ^ (2 << ways[unit.side][step])},
        )

    def start_step(unit, step):
        before = earlier(unit)
        if before is not None:
            step_copy(before, step).wait_send()
        step_copy(unit, step).start()

    lone = batch_count == 2

    def inward_copy(unit, leaf, to_inner):
        _, start = step_size(unit, 0)
        if leaf:
            source = m.mine.at[unit.chunk, pl.ds(start, unit.kept)]
        else:
            source = m.from_outer.at[unit.chunk, unit.rows]
        if to_inner:
            target = m.from_inner.at[unit.chunk, unit.rows]
        else:
            target = m.from_outer.at[unit.chunk, pl.ds(unit.first, unit.kept)]
        return remote(
            source,
            target,
            m.z_send.at[0, unit.place],
            m.z_recv.at[1 if to_inner else 0, unit.place],
            {"batch": inner},
        )

    def outward(unit):
        both = m.from_inner.at[unit.chunk, unit.rows]
        return remote(both, both, m.z_send.at[1, unit.place], m.z_recv.at[1, unit.place], {"batch": outer})

    def start_inward(unit, leaf, to_inner):
        before = earlier(unit)
        if before is not None:
            inward_copy(before, leaf, to_inner).wait_send()
        inward_copy(unit, leaf, to_inner).start()

    def leave(unit):
        @pl.when(jnp.logical_not(has_outer))
        def _():
            start_inward(unit, True, lone)

    def halve(unit, step):
        step_copy(unit, step).wait_recv()
        size, start = step_size(unit, step)
        land = landing(unit, step)
        if step + 1 < bits:
            part = size // 2
            m.mine[unit.chunk, pl.ds(start + part, part), :] += land[pl.ds(part, part), :]
            start_step(unit, step + 1)
            m.mine[unit.chunk, pl.ds(start, part), :] += land[pl.ds(0, part), :]
        else:
            m.mine[unit.chunk, pl.ds(start, size), :] += land[...]
            leave(unit)

    def gather(unit):
        if lone:
            return
        _, start = step_size(unit, 0)
        kept = unit.kept

        @pl.when(has_outer)
        def _():
            inward_copy(unit, True, False).wait_recv()
            if unit.crossed:
                m.from_outer[unit.chunk, pl.ds(kept, kept), :] = m.mine[unit.chunk, pl.ds(start, kept), :]
            else:
                m.from_outer[unit.chunk, pl.ds(unit.first, kept), :] += m.mine[unit.chunk, pl.ds(start, kept), :]

        @pl.when(has_outer & is_inner)
        def _():
            start_inward(unit, False, True)

        if batch_count > 4:

            @pl.when(has_outer & jnp.logical_not(is_inner))
            def _():
                start_inward(unit, False, False)

    def write_out(unit):
        before = earlier(unit)
        if before is not None:
            o_out(before).wait()
        o_out(unit).start()

    def close(unit):
        row = unit.rows
        before = earlier(unit)

        @pl.when(is_inner)
        def _():
            inward_copy(unit, lone, True).wait_recv()
            own = m.mine[unit.chunk, row, :] if lone else m.from_outer[unit.chunk, row, :]
            m.from_inner[unit.chunk, row, :] = (m.from_inner[unit.chunk, row, :] + own) * grad_scale

        @pl.when(is_inner & has_outer)
        def _():
            if before is not None:
                outward(before).wait_send()
            outward(unit).start()

        pl.when(is_inner)(lambda: write_out(unit))

    def take(unit):
        before = earlier(unit)

        @pl.when(jnp.logical_not(is_inner))
        def _():
            inward_copy(unit, lone, True).wait_recv()

        if batch_count > 4:

            @pl.when(jnp.logical_not(is_inner) & has_outer)
            def _():
                if before is not None:
                    outward(before).wait_send()
                outward(unit).start()

        pl.when(jnp.logical_not(is_inner))(lambda: write_out(unit))

    tiles = width // TILE

    def token_tiles(first, count):
        @pl.loop(first, first + count)
        def _(index):
            w_tile(index).wait()

            @pl.when(index >= 2)
            def _():
                t_out(index - 2).wait()

            m.t_tile[index % 2] = dot(m.qkv[...], m.w_tiles[index % 2], 1, 1).astype(m.t_tile.dtype)
            t_out(index).start()

            @pl.when(index + 2 < tiles)
            def _():
                w_tile(index + 2).start()

    def open_place(position):
        assert places[position][0] in ready
        for unit in units_of(position):
            if unit.crossed:
                cross_copy(unit).wait_recv()
                index = CROSS.index(unit.chunk // 2) * 2 + unit.side
                part = half // 4
                upper = pl.ds(part, part)
                m.mine[unit.chunk, upper, :] += m.cross_land[index, upper, :]
                start_step(unit, 0)
                lower = pl.ds(0, part)
                m.mine[unit.chunk, lower, :] += m.cross_land[index, lower, :]
            else:
                start_step(unit, 0)

    events = {}
    for position in range(len(places)):
        for order, unit in enumerate(units_of(position)):
            stages = [functools.partial(halve, unit, step) for step in range(bits)]
            for number, stage in enumerate(stages):
                events.setdefault(position + number, []).append((0, -number, order, stage))
            late = EARLY_LAGS if position < EARLY else (MID_LAGS if unit.count == 1 else LAST_LAGS)
            for number, (stage, lag) in enumerate(zip((gather, close, take), late)):
                events.setdefault(position + bits + lag, []).append(
                    (1, -number, order, functools.partial(stage, unit))
                )

    def run_events(slot):
        for _, _, _, event in sorted(events.get(slot, []), key=lambda item: item[:3]):
            event()

    x_in.wait()
    project(0)
    c_in.wait()
    pl.semaphore_wait(barrier, bits + 2 + has_outer.astype(jnp.int32))
    make_states(0)
    turn_tokens(0, 1)
    chain(0, 1)
    turn_tokens(1, chips)
    project(1)
    make_states(1)
    in_block(0, 0, 1)
    chain(0, 1)
    in_block(0, 1, 1)
    chain(1, 1)
    chain(0)
    finish(0)
    join_tokens()
    chain(1, 1)
    multiply(0)
    open_place(0)
    multiply(1)
    open_place(1)
    multiply(2)
    chain(1)
    for index in range(2):
        w_tile(index).start()
    for group in (2, 3):
        project(group)
        make_states(group)
    chain(2, 1)
    chain(3, 1)
    ahead = {
        1: [
            lambda: in_block(1),
            lambda: finish(1),
            lambda: multiply(3),
            lambda: open_place(2),
            lambda: multiply(4),
            lambda: multiply(5),
        ],
    }
    opens = {0: [], 1: [3]}
    after = {
        1: [lambda: in_block(2), lambda: chain(2, 1), lambda: chain(3, 1)],
        2: [lambda: chain(2), lambda: chain(3)],
        3: [lambda: finish(2), lambda: in_block(3), lambda: multiply(6)],
        4: [lambda: multiply(7), lambda: multiply(8)],
        5: [lambda: finish(3)],
        6: [lambda: multiply(9), lambda: multiply(10)],
        7: [lambda: multiply(11)],
    }
    for index in range(tiles // 2):
        after.setdefault(8 + index, []).append(functools.partial(token_tiles, 2 * index, 2))
    for slot in range(max(max(events), max(after)) + 1):
        for task in ahead.get(slot, []):
            task()
        run_events(slot)
        for position in opens.get(slot, [slot + 2]):
            if position < len(places):
                open_place(position)
        for task in after.get(slot, []):
            task()

    for index in range(tiles - 2, tiles):
        t_out(index).wait()
    for group in range(groups):
        a_out(group).wait()
        first_swap(group).wait_send()
        last_swap(group).wait_send()
        for bit in range(bits):
            if bit == bits - 1:
                pl.when(jnp.logical_not(takes(bit)))(bit_swap(group, bit).wait_send)
            else:
                bit_swap(group, bit).wait_send()
        if group >= groups - 2:
            for spot in range(6):
                grad_swap(group, spot).wait_send()
    for position in range(len(places)):
        for unit in units_of(position):
            if unit.crossed:
                cross_copy(unit).wait_send()
            if position < len(places) - PLACES:
                continue
            for step in range(bits):
                step_copy(unit, step).wait_send()
            if lone:
                inward_copy(unit, True, True).wait_send()
            else:

                @pl.when(jnp.logical_not(has_outer))
                def _():
                    inward_copy(unit, True, False).wait_send()

                @pl.when(has_outer & is_inner)
                def _():
                    inward_copy(unit, False, True).wait_send()

                if batch_count > 4:

                    @pl.when(has_outer & jnp.logical_not(is_inner))
                    def _():
                        inward_copy(unit, False, False).wait_send()

                @pl.when(has_outer)
                def _():
                    outward(unit).wait_send()

            o_out(unit).wait()


def body(tokens, w_qkv, cotangent):
    rows, width = tokens.shape[1:]
    columns = w_qkv.shape[1]
    head_width = columns // 3
    assert rows == BLK and head_width == HEADS * DH
    seq_count = lax.axis_size("seq")
    batch_count = lax.axis_size("batch")
    bits = bits_of(seq_count) - 1
    groups = head_width // PAIR
    chunks = columns // COLS
    half = width // 2
    own_rows = width // seq_count
    crossed = max(2 * len(CROSS), 1)
    places = 2 * PLACES
    grad_scale = float(batch_count * seq_count * rows) ** -0.5
    f32, bf16 = jnp.float32, jnp.bfloat16
    state = (2, DH, DH)
    sizes = dict(
        x_all=pltpu.VMEM((rows, width), bf16),
        x_cat=pltpu.VMEM((half, 2 * rows), bf16),
        turned=pltpu.VMEM((2 * own_rows, rows), bf16),
        w_parts=pltpu.VMEM((3, width, PAIR), bf16),
        w_tiles=pltpu.VMEM((2, TILE, columns), bf16),
        t_tile=pltpu.VMEM((2, rows, TILE), bf16),
        qkv=pltpu.VMEM((rows, columns), bf16),
        grads=pltpu.VMEM((rows, head_width), bf16),
        scale=pltpu.VMEM((rows, COLS), f32),
        parts=pltpu.VMEM((4, rows, PAIR), f32),
        tri=pltpu.VMEM((3, TILE, TILE), bf16),
        states=pltpu.VMEM((groups, 2) + state, f32),
        mates=pltpu.VMEM((groups,) + state, f32),
        gives=pltpu.VMEM((groups,) + state, f32),
        totals=pltpu.VMEM((bits, groups) + state, f32),
        others=pltpu.VMEM((bits, groups) + state, f32),
        carry=pltpu.VMEM((groups, 2) + state, f32),
        g_send=pltpu.VMEM((2, 6, rows, COLS), f32),
        g_land=pltpu.VMEM((2, 6, rows, COLS), f32),
        g_cat=pltpu.VMEM((3, 2 * rows, PAIR), bf16),
        mine=pltpu.VMEM((chunks, half, COLS), f32),
        lands=[pltpu.VMEM((places, half >> (step + 1), COLS), f32) for step in range(bits)],
        cross_land=pltpu.VMEM((crossed, half // 2, COLS), f32),
        from_outer=pltpu.VMEM((chunks, own_rows, COLS), f32),
        from_inner=pltpu.VMEM((chunks, own_rows, COLS), f32),
        w_sem=pltpu.SemaphoreType.DMA((3,)),
        x_sem=pltpu.SemaphoreType.DMA((2,)),
        x_send=pltpu.SemaphoreType.DMA((1 << bits,)),
        x_recv=pltpu.SemaphoreType.DMA((1 << bits,)),
        t_sem=pltpu.SemaphoreType.DMA((4,)),
        a_sem=pltpu.SemaphoreType.DMA((groups,)),
        o_sem=pltpu.SemaphoreType.DMA((places,)),
        swap_send=pltpu.SemaphoreType.DMA((2, groups)),
        swap_recv=pltpu.SemaphoreType.DMA((2, groups)),
        bit_send=pltpu.SemaphoreType.DMA((bits, groups)),
        bit_recv=pltpu.SemaphoreType.DMA((bits, groups)),
        g_ssem=pltpu.SemaphoreType.DMA((2, 6)),
        g_rsem=pltpu.SemaphoreType.DMA((2, 6)),
        cross_send=pltpu.SemaphoreType.DMA((crossed,)),
        cross_recv=pltpu.SemaphoreType.DMA((crossed,)),
        step_send=pltpu.SemaphoreType.DMA((bits, places)),
        step_recv=pltpu.SemaphoreType.DMA((bits, places)),
        z_send=pltpu.SemaphoreType.DMA((2, places)),
        z_recv=pltpu.SemaphoreType.DMA((2, places)),
    )
    attended, token_grad, weight_grad = pl.pallas_call(
        functools.partial(step_kernel, seq_count, batch_count, grad_scale, tuple(sizes)),
        out_shape=(
            jax.ShapeDtypeStruct((rows, head_width), bf16),
            jax.ShapeDtypeStruct((rows, width), bf16),
            jax.ShapeDtypeStruct((own_rows, columns), f32),
        ),
        in_specs=[pl.BlockSpec(memory_space=pl.ANY)] * 3,
        out_specs=[pl.BlockSpec(memory_space=pl.ANY)] * 3,
        scratch_shapes=list(sizes.values()),
        compiler_params=pltpu.CompilerParams(
            collective_id=0, has_side_effects=True, vmem_limit_bytes=60 * 1024 * 1024
        ),
    )(tokens[0], w_qkv, cotangent[0])
    return attended[None], token_grad[None], weight_grad


def solution(mesh):
    return jax.shard_map(
        body,
        mesh=mesh,
        in_specs=(P("batch", "seq", None), P(), P("batch", "seq", None)),
        out_specs=(P("batch", "seq", None), P("batch", "seq", None), P("seq", None)),
        check_vma=False,
    )
```

```python
import functools
import types

import jax
import jax.numpy as jnp
from jax import lax
from jax.experimental import pallas as pl
from jax.experimental.pallas import tpu as pltpu
from jax.sharding import PartitionSpec as P

HEADS = 8
DH = 128
BLK = 512
COLS = 128
PAIR = 2 * COLS
TILE = 256
MESH = pl.DeviceIdType.MESH
CROSS = (2, 5)
SEQUENCE = (0, 1, 3, 2, 4, 5, 6, 7, 8, 9, 10, 11)
PLACES = 6
SPLIT = {10: 2, 11: 2}
EARLY = 4
EARLY_LAGS = (1, 2, 3)
MID_LAGS = (0, 1, 3)
LAST_LAGS = (0, 2, 4)


def bits_of(count):
    bits = count.bit_length() - 1
    assert count == 1 << bits
    return bits


def dot(left, right, left_dim, right_dim):
    return lax.dot_general(
        left, right, (((left_dim,), (right_dim,)), ((), ())), preferred_element_type=jnp.float32
    )


def wide(left, state, state_dim):
    high = state.astype(jnp.bfloat16)
    rest = (state - high.astype(jnp.float32)).astype(jnp.bfloat16)
    return dot(left, high, 1, state_dim) + dot(left, rest, 1, state_dim)


def lanes(start, size):
    return pl.ds(pl.multiple_of(start, COLS), size)


def step_kernel(seq_count, batch_count, grad_scale, names, x_hbm, w_hbm, c_hbm, a_hbm, t_hbm, o_hbm, *scratch):
    m = types.SimpleNamespace(**dict(zip(names, scratch)))
    bits = bits_of(seq_count) - 1
    chips = 1 << bits
    rows, width = x_hbm.shape
    head_width = c_hbm.shape[1]
    groups = head_width // PAIR
    pairs = 3 * groups
    chunks = 2 * pairs
    half = width // 2
    own_rows = width // seq_count
    rank = lax.axis_index("seq")
    core = rank % 2
    chip = rank // 2
    plane = lax.axis_index("batch")
    middle = batch_count // 2
    low_side = plane < middle
    depth = jnp.where(low_side, middle - 1 - plane, plane - middle)
    has_outer = jnp.where(low_side, plane > 0, plane < batch_count - 1)
    is_inner = depth == 0
    inner = jnp.where(low_side, plane + 1, plane - 1)
    outer = jnp.where(low_side, plane - 1, plane + 1)
    mate_id = {"seq": rank ^ 1}

    base = list(range(bits))
    turned = base[bits // 2 :] + base[: bits // 2]
    ways = [base, turned]
    crossed = set(CROSS) if batch_count == 4 else set()
    assert sorted(SEQUENCE) == list(range(pairs))
    places = [(pair, sub) for pair in SEQUENCE for sub in range(SPLIT.get(pair, 1))]

    def units_of(position):
        pair, sub = places[position]
        count = SPLIT.get(pair, 1)
        return [
            types.SimpleNamespace(
                position=position,
                chunk=2 * pair + side,
                side=side,
                sub=sub,
                count=count,
                crossed=pair in crossed,
                place=(position % PLACES) * 2 + side,
                kept=own_rows // 2 if pair in crossed else own_rows // count,
                rows=pl.ds(sub * (own_rows // count), own_rows // count),
                first=sub * (own_rows // count),
            )
            for side in range(2)
        ]

    def earlier(unit):
        if unit.position < PLACES:
            return None
        return units_of(unit.position - PLACES)[unit.side]

    def local(source, target, sem):
        return pltpu.make_async_copy(source, target, sem)

    def remote(source, target, send, recv, device):
        return pltpu.make_async_remote_copy(
            src_ref=source, dst_ref=target, send_sem=send, recv_sem=recv, device_id=device, device_id_type=MESH
        )

    def w_part(group, part):
        column = lanes(part * head_width + group * PAIR, PAIR)
        return local(w_hbm.at[:, column], m.w_parts.at[part], m.w_sem.at[part])

    def w_tile(index):
        row = pl.ds(pl.multiple_of(index * TILE, TILE), TILE)
        return local(w_hbm.at[row], m.w_tiles.at[index % 2], m.t_sem.at[index % 2])

    def t_out(index):
        return local(m.t_tile.at[index % 2], t_hbm.at[:, lanes(index * TILE, TILE)], m.t_sem.at[2 + index % 2])

    def a_out(group):
        column = pl.ds(group * PAIR, PAIR)
        return local(m.grads.at[:, column], a_hbm.at[:, column], m.a_sem.at[group])

    def o_out(unit):
        group, spot = unit.chunk // 6, unit.chunk % 6
        column = (spot % 3) * head_width + group * PAIR + (spot // 3) * COLS
        row = unit.rows
        return local(m.from_inner.at[unit.chunk, row], o_hbm.at[row, pl.ds(column, COLS)], m.o_sem.at[unit.place])

    x_in = local(x_hbm, m.x_all, m.x_sem.at[0])
    c_in = local(c_hbm, m.grads, m.x_sem.at[1])
    for part in range(3):
        w_part(0, part).start()
        if part == 0:
            x_in.start()
    c_in.start()
    barrier = pltpu.get_barrier_semaphore()
    pl.semaphore_signal(barrier, inc=1, device_id=mate_id, device_id_type=MESH)
    for bit in range(bits):
        pl.semaphore_signal(barrier, inc=1, device_id={"seq": rank ^ (2 << bit)}, device_id_type=MESH)
    pl.semaphore_signal(barrier, inc=1, device_id={"batch": inner}, device_id_type=MESH)

    @pl.when(has_outer)
    def _():
        pl.semaphore_signal(barrier, inc=1, device_id={"batch": outer}, device_id_type=MESH)

    position = rank * rows + lax.broadcasted_iota(jnp.int32, (rows, COLS), 0)
    m.scale[...] = DH ** (-0.5) / jnp.sqrt(position.astype(jnp.float32) + 1.0)

    def project(group):
        @pl.loop(0, 3)
        def _(part):
            w_part(group, part).wait()
            m.qkv[:, lanes(part * head_width + group * PAIR, PAIR)] = dot(
                m.x_all[...], m.w_parts[part], 1, 0
            ).astype(m.qkv.dtype)
            if group + 1 < groups:
                w_part(group + 1, part).start()

    def head_columns(group, head):
        start = group * PAIR + head * DH
        return [lanes(part * head_width + start, DH) for part in range(3)] + [lanes(start, DH)]

    def first_swap(group):
        return remote(
            m.states.at[group, 1 - core], m.mates.at[group], m.swap_send.at[0, group], m.swap_recv.at[0, group], mate_id
        )

    def last_swap(group):
        return remote(
            m.gives.at[group], m.carry.at[group, core], m.swap_send.at[1, group], m.swap_recv.at[1, group], mate_id
        )

    def bit_swap(group, bit):
        return remote(
            m.totals.at[bit, group],
            m.others.at[bit, group],
            m.bit_send.at[bit, group],
            m.bit_recv.at[bit, group],
            {"seq": rank ^ (2 << bit)},
        )

    def takes(bit):
        return ((chip // (1 << bit)) % 2) != core

    def make_states(group):
        @pl.loop(0, 2)
        def _(head):
            q_at, k_at, v_at, g_at = head_columns(group, head)
            grad = (m.grads[:, g_at].astype(jnp.float32) * m.scale[...]).astype(jnp.bfloat16)
            m.grads[:, g_at] = grad
            m.states[group, 0, head] = dot(m.qkv[:, k_at], m.qkv[:, v_at], 0, 0)
            m.states[group, 1, head] = dot(m.qkv[:, q_at], grad, 0, 0)

        first_swap(group).start()

    def start_bit(group, bit):
        if bit == bits - 1:
            pl.when(jnp.logical_not(takes(bit)))(bit_swap(group, bit).start)
        else:
            bit_swap(group, bit).start()

    def chain_first(group):
        first_swap(group).wait_recv()
        m.totals[0, group] = m.states[group, core] + m.mates[group]
        start_bit(group, 0)
        m.carry[group, core] = jnp.zeros(m.mates.shape[1:], jnp.float32)

    def chain_bit(group, bit):
        last = bit == bits - 1
        if not last:
            bit_swap(group, bit).wait_recv()
            m.totals[bit + 1, group] = m.totals[bit, group] + m.others[bit, group]
            start_bit(group, bit + 1)

        @pl.when(takes(bit))
        def _():
            if last:
                bit_swap(group, bit).wait_recv()
            m.carry[group, core] += m.others[bit, group]

        if last:
            m.gives[group] = m.carry[group, core] + m.states[group, core]
            last_swap(group).start()

    chains = [
        [functools.partial(chain_first, group)] + [functools.partial(chain_bit, group, bit) for bit in range(bits)]
        for group in range(groups)
    ]

    def chain(group, count=None):
        count = len(chains[group]) if count is None else count
        for _ in range(min(count, len(chains[group]))):
            chains[group].pop(0)()

    def in_block(group, first=0, count=2):
        low = slice(0, TILE)
        high = slice(TILE, BLK)
        row = lax.broadcasted_iota(jnp.int32, (TILE, TILE), 0)
        col = lax.broadcasted_iota(jnp.int32, (TILE, TILE), 1)
        causal = row >= col

        @pl.loop(first, first + count)
        def _(head):
            q_at, k_at, v_at, g_at = head_columns(group, head)
            out_at = lanes(head * DH, DH)

            def products(left_ref, left_at, right_at):
                def one(i, j, masked):
                    value = dot(left_ref[i, left_at], m.qkv[j, right_at], 1, 1)
                    if masked:
                        value = jnp.where(causal, value, 0.0)
                    return value.astype(jnp.bfloat16)

                m.tri[0] = one(low, low, True)
                m.tri[1] = one(high, low, False)
                m.tri[2] = one(high, high, True)

            def by_rows(index, ref, at):
                m.parts[index, low, out_at] = dot(m.tri[0], ref[low, at], 1, 0)
                m.parts[index, high, out_at] = dot(m.tri[1], ref[low, at], 1, 0) + dot(m.tri[2], ref[high, at], 1, 0)

            def by_columns(index, ref, at):
                m.parts[index, low, out_at] = dot(m.tri[0], ref[low, at], 0, 0) + dot(m.tri[1], ref[high, at], 0, 0)
                m.parts[index, high, out_at] = dot(m.tri[2], ref[high, at], 0, 0)

            products(m.qkv, q_at, k_at)
            by_rows(0, m.qkv, v_at)
            by_columns(3, m.grads, g_at)
            products(m.grads, g_at, v_at)
            by_rows(1, m.qkv, k_at)
            by_columns(2, m.qkv, q_at)

    def grad_swap(group, spot):
        slot = group % 2
        return remote(
            m.g_send.at[slot, spot],
            m.g_land.at[slot, spot],
            m.g_ssem.at[slot, spot],
            m.g_rsem.at[slot, spot],
            mate_id,
        )

    def finish(group):
        slot = group % 2
        last_swap(group).wait_recv()

        @pl.loop(0, 2)
        def _(head):
            q_at, k_at, v_at, g_at = head_columns(group, head)
            out_at = lanes(head * DH, DH)
            query, key, value, grad = m.qkv[:, q_at], m.qkv[:, k_at], m.qkv[:, v_at], m.grads[:, g_at]
            kv, gs = m.carry[group, 0, head], m.carry[group, 1, head]

            def give(part, at, result):
                spot = 3 * head + part
                low = result.astype(jnp.bfloat16)
                m.qkv[:, at] = low
                m.g_cat[spot // 2, 0:rows, lanes(spot % 2 * COLS, COLS)] = low
                if group >= 2:
                    grad_swap(group - 2, spot).wait_send()
                m.g_send[slot, spot] = low.astype(jnp.float32)
                grad_swap(group, spot).start()

            give(0, q_at, m.parts[1, :, out_at] + wide(grad, kv, 1))
            give(1, k_at, m.parts[2, :, out_at] + wide(value, gs, 1))
            give(2, v_at, m.parts[3, :, out_at] + wide(key, gs, 0))
            attended = (m.parts[0, :, out_at] + wide(query, kv, 0)) * m.scale[...]
            m.grads[:, g_at] = attended.astype(jnp.bfloat16)

        a_out(group).start()

    spare = rows // COLS

    def x_swap(index):
        row = pl.ds(pl.multiple_of(index * own_rows, own_rows), own_rows)
        return remote(
            m.mine.at[pl.ds(chunks - spare, spare), row],
            m.mine.at[pl.ds(chunks - 2 * spare, spare), row],
            m.x_send.at[index],
            m.x_recv.at[index],
            mate_id,
        )

    def turn_tokens(first, last):
        @pl.loop(first, last)
        def _(index):
            owner = chip ^ index
            m.turned[...] = m.x_all[:, lanes(owner * 2 * own_rows, 2 * own_rows)].T
            row = pl.ds(pl.multiple_of(index * own_rows, own_rows), own_rows)
            m.x_cat[row, 0:rows] = m.turned[pl.ds(pl.multiple_of(core * own_rows, own_rows), own_rows), :]
            other = m.turned[pl.ds(pl.multiple_of((1 - core) * own_rows, own_rows), own_rows), :]
            for piece in range(spare):
                m.mine[chunks - spare + piece, row, :] = other[:, piece * COLS : (piece + 1) * COLS].astype(jnp.float32)
            x_swap(index).start()

    def join_tokens():
        @pl.loop(0, chips)
        def _(index):
            x_swap(index).wait_recv()
            row = pl.ds(pl.multiple_of(index * own_rows, own_rows), own_rows)
            for piece in range(spare):
                at = rows + piece * COLS
                m.x_cat[row, at : at + COLS] = m.mine[chunks - 2 * spare + piece, row, :].astype(jnp.bfloat16)

    keeps_low = jnp.where(is_inner, 0, 1)

    ready = set()

    def multiply(pair):
        group = pair // 3
        ready.add(pair)
        for side in range(2):
            spot = 2 * (pair % 3) + side
            grad_swap(group, spot).wait_recv()
            m.g_cat[spot // 2, rows : 2 * rows, side * COLS : (side + 1) * COLS] = m.g_land[group % 2, spot].astype(
                jnp.bfloat16
            )
        if pair == (chunks - spare) // 2:
            for index in range(chips):
                x_swap(index).wait_send()
        count = 2 if pair in crossed else SPLIT.get(pair, 1)

        @pl.loop(0, chips)
        def _(index):
            value = dot(
                m.x_cat[pl.ds(pl.multiple_of(index * own_rows, own_rows), own_rows), :], m.g_cat[pair % 3], 1, 0
            )
            for side, way in enumerate(ways):
                spot = sum((index // (1 << bit) % 2) * (1 << (bits - 1 - k)) for k, bit in enumerate(way))
                part_rows = own_rows // count
                for sub in range(count):
                    block = sub
                    if pair in crossed:
                        block = 1 - keeps_low if sub == 0 else keeps_low
                    row = pl.multiple_of((block * chips + spot) * part_rows, part_rows)
                    m.mine[2 * pair + side, pl.ds(row, part_rows), :] = value[
                        sub * part_rows : (sub + 1) * part_rows, side * COLS : (side + 1) * COLS
                    ]

        if pair in crossed:
            for unit in units_of(places.index((pair, 0))):
                cross_copy(unit).start()

    def cross_copy(unit):
        index = CROSS.index(unit.chunk // 2) * 2 + unit.side
        return remote(
            m.mine.at[unit.chunk, pl.ds(half // 2, half // 2)],
            m.cross_land.at[index],
            m.cross_send.at[index],
            m.cross_recv.at[index],
            {"batch": plane ^ 1},
        )

    def step_size(unit, step):
        whole = half // 2 if unit.crossed else half // unit.count
        return whole >> (step + 1), unit.sub * whole

    def landing(unit, step):
        size, _ = step_size(unit, step)
        return m.lands[step].at[unit.place, pl.ds(0, size)]

    def step_copy(unit, step):
        size, start = step_size(unit, step)
        return remote(
            m.mine.at[unit.chunk, pl.ds(start + size, size)],
            landing(unit, step),
            m.step_send.at[step, unit.place],
            m.step_recv.at[step, unit.place],
            {"seq": rank ^ (2 << ways[unit.side][step])},
        )

    def start_step(unit, step):
        before = earlier(unit)
        if before is not None:
            step_copy(before, step).wait_send()
        step_copy(unit, step).start()

    lone = batch_count == 2

    def inward_copy(unit, leaf, to_inner):
        _, start = step_size(unit, 0)
        if leaf:
            source = m.mine.at[unit.chunk, pl.ds(start, unit.kept)]
        else:
            source = m.from_outer.at[unit.chunk, unit.rows]
        if to_inner:
            target = m.from_inner.at[unit.chunk, unit.rows]
        else:
            target = m.from_outer.at[unit.chunk, pl.ds(unit.first, unit.kept)]
        return remote(
            source,
            target,
            m.z_send.at[0, unit.place],
            m.z_recv.at[1 if to_inner else 0, unit.place],
            {"batch": inner},
        )

    def outward(unit):
        both = m.from_inner.at[unit.chunk, unit.rows]
        return remote(both, both, m.z_send.at[1, unit.place], m.z_recv.at[1, unit.place], {"batch": outer})

    def start_inward(unit, leaf, to_inner):
        before = earlier(unit)
        if before is not None:
            inward_copy(before, leaf, to_inner).wait_send()
        inward_copy(unit, leaf, to_inner).start()

    def leave(unit):
        @pl.when(jnp.logical_not(has_outer))
        def _():
            start_inward(unit, True, lone)

    def halve(unit, step):
        step_copy(unit, step).wait_recv()
        size, start = step_size(unit, step)
        land = landing(unit, step)
        if step + 1 < bits:
            part = size // 2
            m.mine[unit.chunk, pl.ds(start + part, part), :] += land[pl.ds(part, part), :]
            start_step(unit, step + 1)
            m.mine[unit.chunk, pl.ds(start, part), :] += land[pl.ds(0, part), :]
        else:
            m.mine[unit.chunk, pl.ds(start, size), :] += land[...]
            leave(unit)

    def gather(unit):
        if lone:
            return
        _, start = step_size(unit, 0)
        kept = unit.kept

        @pl.when(has_outer)
        def _():
            inward_copy(unit, True, False).wait_recv()
            if unit.crossed:
                m.from_outer[unit.chunk, pl.ds(kept, kept), :] = m.mine[unit.chunk, pl.ds(start, kept), :]
            else:
                m.from_outer[unit.chunk, pl.ds(unit.first, kept), :] += m.mine[unit.chunk, pl.ds(start, kept), :]

        @pl.when(has_outer & is_inner)
        def _():
            start_inward(unit, False, True)

        if batch_count > 4:

            @pl.when(has_outer & jnp.logical_not(is_inner))
            def _():
                start_inward(unit, False, False)

    def write_out(unit):
        before = earlier(unit)
        if before is not None:
            o_out(before).wait()
        o_out(unit).start()

    def close(unit):
        row = unit.rows
        before = earlier(unit)

        @pl.when(is_inner)
        def _():
            inward_copy(unit, lone, True).wait_recv()
            own = m.mine[unit.chunk, row, :] if lone else m.from_outer[unit.chunk, row, :]
            m.from_inner[unit.chunk, row, :] = (m.from_inner[unit.chunk, row, :] + own) * grad_scale

        @pl.when(is_inner & has_outer)
        def _():
            if before is not None:
                outward(before).wait_send()
            outward(unit).start()

        pl.when(is_inner)(lambda: write_out(unit))

    def take(unit):
        before = earlier(unit)

        @pl.when(jnp.logical_not(is_inner))
        def _():
            inward_copy(unit, lone, True).wait_recv()

        if batch_count > 4:

            @pl.when(jnp.logical_not(is_inner) & has_outer)
            def _():
                if before is not None:
                    outward(before).wait_send()
                outward(unit).start()

        pl.when(jnp.logical_not(is_inner))(lambda: write_out(unit))

    tiles = width // TILE

    def token_tiles(first, count):
        @pl.loop(first, first + count)
        def _(index):
            w_tile(index).wait()

            @pl.when(index >= 2)
            def _():
                t_out(index - 2).wait()

            m.t_tile[index % 2] = dot(m.qkv[...], m.w_tiles[index % 2], 1, 1).astype(m.t_tile.dtype)
            t_out(index).start()

            @pl.when(index + 2 < tiles)
            def _():
                w_tile(index + 2).start()

    def open_place(position):
        assert places[position][0] in ready
        for unit in units_of(position):
            if unit.crossed:
                cross_copy(unit).wait_recv()
                index = CROSS.index(unit.chunk // 2) * 2 + unit.side
                part = half // 4
                upper = pl.ds(part, part)
                m.mine[unit.chunk, upper, :] += m.cross_land[index, upper, :]
                start_step(unit, 0)
                lower = pl.ds(0, part)
                m.mine[unit.chunk, lower, :] += m.cross_land[index, lower, :]
            else:
                start_step(unit, 0)

    events = {}
    for position in range(len(places)):
        for order, unit in enumerate(units_of(position)):
            stages = [functools.partial(halve, unit, step) for step in range(bits)]
            for number, stage in enumerate(stages):
                events.setdefault(position + number, []).append((0, -number, order, stage))
            late = EARLY_LAGS if position < EARLY else (MID_LAGS if unit.count == 1 else LAST_LAGS)
            for number, (stage, lag) in enumerate(zip((gather, close, take), late)):
                events.setdefault(position + bits + lag, []).append(
                    (1, number, order, functools.partial(stage, unit))
                )

    def run_events(slot):
        for _, _, _, event in sorted(events.get(slot, []), key=lambda item: item[:3]):
            event()

    x_in.wait()
    project(0)
    c_in.wait()
    pl.semaphore_wait(barrier, bits + 2 + has_outer.astype(jnp.int32))
    make_states(0)
    turn_tokens(0, 1)
    chain(0, 1)
    turn_tokens(1, chips)
    project(1)
    make_states(1)
    in_block(0, 0, 1)
    chain(0, 1)
    in_block(0, 1, 1)
    chain(1, 1)
    chain(0)
    finish(0)
    join_tokens()
    chain(1, 1)
    multiply(0)
    open_place(0)
    multiply(1)
    open_place(1)
    multiply(2)
    chain(1)
    for index in range(2):
        w_tile(index).start()
    project(2)
    make_states(2)
    project(3)
    run_events(0)
    make_states(3)
    chain(2, 1)
    chain(3, 1)
    ahead = {
        1: [
            lambda: in_block(1),
            lambda: finish(1),
            lambda: multiply(3),
            lambda: open_place(2),
            lambda: multiply(4),
            lambda: multiply(5),
        ],
    }
    opens = {0: [], 1: [3]}
    after = {
        1: [lambda: in_block(2), lambda: chain(2, 1), lambda: chain(3, 1)],
        2: [lambda: chain(2), lambda: chain(3)],
        3: [lambda: finish(2), lambda: in_block(3), lambda: multiply(6)],
        4: [lambda: multiply(7), lambda: multiply(8)],
        5: [lambda: finish(3)],
        6: [lambda: multiply(9), lambda: multiply(10)],
        7: [lambda: multiply(11)],
    }
    for index in range(tiles // 2):
        after.setdefault(8 + index, []).append(functools.partial(token_tiles, 2 * index, 2))
    for slot in range(max(max(events), max(after)) + 1):
        for task in ahead.get(slot, []):
            task()
        if slot:
            run_events(slot)
        for position in opens.get(slot, [slot + 2]):
            if position < len(places):
                open_place(position)
        for task in after.get(slot, []):
            task()

    for index in range(tiles - 2, tiles):
        t_out(index).wait()
    for group in range(groups):
        a_out(group).wait()
        first_swap(group).wait_send()
        last_swap(group).wait_send()
        for bit in range(bits):
            if bit == bits - 1:
                pl.when(jnp.logical_not(takes(bit)))(bit_swap(group, bit).wait_send)
            else:
                bit_swap(group, bit).wait_send()
        if group >= groups - 2:
            for spot in range(6):
                grad_swap(group, spot).wait_send()
    for position in range(len(places)):
        for unit in units_of(position):
            if unit.crossed:
                cross_copy(unit).wait_send()
            if position < len(places) - PLACES:
                continue
            for step in range(bits):
                step_copy(unit, step).wait_send()
            if lone:
                inward_copy(unit, True, True).wait_send()
            else:

                @pl.when(jnp.logical_not(has_outer))
                def _():
                    inward_copy(unit, True, False).wait_send()

                @pl.when(has_outer & is_inner)
                def _():
                    inward_copy(unit, False, True).wait_send()

                if batch_count > 4:

                    @pl.when(has_outer & jnp.logical_not(is_inner))
                    def _():
                        inward_copy(unit, False, False).wait_send()

                @pl.when(has_outer)
                def _():
                    outward(unit).wait_send()

            o_out(unit).wait()


def body(tokens, w_qkv, cotangent):
    rows, width = tokens.shape[1:]
    columns = w_qkv.shape[1]
    head_width = columns // 3
    assert rows == BLK and head_width == HEADS * DH
    seq_count = lax.axis_size("seq")
    batch_count = lax.axis_size("batch")
    bits = bits_of(seq_count) - 1
    groups = head_width // PAIR
    chunks = columns // COLS
    half = width // 2
    own_rows = width // seq_count
    crossed = max(2 * len(CROSS), 1)
    places = 2 * PLACES
    grad_scale = float(batch_count * seq_count * rows) ** -0.5
    f32, bf16 = jnp.float32, jnp.bfloat16
    state = (2, DH, DH)
    sizes = dict(
        x_all=pltpu.VMEM((rows, width), bf16),
        x_cat=pltpu.VMEM((half, 2 * rows), bf16),
        turned=pltpu.VMEM((2 * own_rows, rows), bf16),
        w_parts=pltpu.VMEM((3, width, PAIR), bf16),
        w_tiles=pltpu.VMEM((2, TILE, columns), bf16),
        t_tile=pltpu.VMEM((2, rows, TILE), bf16),
        qkv=pltpu.VMEM((rows, columns), bf16),
        grads=pltpu.VMEM((rows, head_width), bf16),
        scale=pltpu.VMEM((rows, COLS), f32),
        parts=pltpu.VMEM((4, rows, PAIR), f32),
        tri=pltpu.VMEM((3, TILE, TILE), bf16),
        states=pltpu.VMEM((groups, 2) + state, f32),
        mates=pltpu.VMEM((groups,) + state, f32),
        gives=pltpu.VMEM((groups,) + state, f32),
        totals=pltpu.VMEM((bits, groups) + state, f32),
        others=pltpu.VMEM((bits, groups) + state, f32),
        carry=pltpu.VMEM((groups, 2) + state, f32),
        g_send=pltpu.VMEM((2, 6, rows, COLS), f32),
        g_land=pltpu.VMEM((2, 6, rows, COLS), f32),
        g_cat=pltpu.VMEM((3, 2 * rows, PAIR), bf16),
        mine=pltpu.VMEM((chunks, half, COLS), f32),
        lands=[pltpu.VMEM((places, half >> (step + 1), COLS), f32) for step in range(bits)],
        cross_land=pltpu.VMEM((crossed, half // 2, COLS), f32),
        from_outer=pltpu.VMEM((chunks, own_rows, COLS), f32),
        from_inner=pltpu.VMEM((chunks, own_rows, COLS), f32),
        w_sem=pltpu.SemaphoreType.DMA((3,)),
        x_sem=pltpu.SemaphoreType.DMA((2,)),
        x_send=pltpu.SemaphoreType.DMA((1 << bits,)),
        x_recv=pltpu.SemaphoreType.DMA((1 << bits,)),
        t_sem=pltpu.SemaphoreType.DMA((4,)),
        a_sem=pltpu.SemaphoreType.DMA((groups,)),
        o_sem=pltpu.SemaphoreType.DMA((places,)),
        swap_send=pltpu.SemaphoreType.DMA((2, groups)),
        swap_recv=pltpu.SemaphoreType.DMA((2, groups)),
        bit_send=pltpu.SemaphoreType.DMA((bits, groups)),
        bit_recv=pltpu.SemaphoreType.DMA((bits, groups)),
        g_ssem=pltpu.SemaphoreType.DMA((2, 6)),
        g_rsem=pltpu.SemaphoreType.DMA((2, 6)),
        cross_send=pltpu.SemaphoreType.DMA((crossed,)),
        cross_recv=pltpu.SemaphoreType.DMA((crossed,)),
        step_send=pltpu.SemaphoreType.DMA((bits, places)),
        step_recv=pltpu.SemaphoreType.DMA((bits, places)),
        z_send=pltpu.SemaphoreType.DMA((2, places)),
        z_recv=pltpu.SemaphoreType.DMA((2, places)),
    )
    attended, token_grad, weight_grad = pl.pallas_call(
        functools.partial(step_kernel, seq_count, batch_count, grad_scale, tuple(sizes)),
        out_shape=(
            jax.ShapeDtypeStruct((rows, head_width), bf16),
            jax.ShapeDtypeStruct((rows, width), bf16),
            jax.ShapeDtypeStruct((own_rows, columns), f32),
        ),
        in_specs=[pl.BlockSpec(memory_space=pl.ANY)] * 3,
        out_specs=[pl.BlockSpec(memory_space=pl.ANY)] * 3,
        scratch_shapes=list(sizes.values()),
        compiler_params=pltpu.CompilerParams(
            collective_id=0, has_side_effects=True, vmem_limit_bytes=60 * 1024 * 1024
        ),
    )(tokens[0], w_qkv, cotangent[0])
    return attended[None], token_grad[None], weight_grad


def solution(mesh):
    return jax.shard_map(
        body,
        mesh=mesh,
        in_specs=(P("batch", "seq", None), P(), P("batch", "seq", None)),
        out_specs=(P("batch", "seq", None), P("batch", "seq", None), P("seq", None)),
        check_vma=False,
    )
```

```python
import functools
import types

import jax
import jax.numpy as jnp
from jax import lax
from jax.experimental import pallas as pl
from jax.experimental.pallas import tpu as pltpu
from jax.sharding import PartitionSpec as P

HEADS = 8
DH = 128
BLK = 512
COLS = 128
PAIR = 2 * COLS
TILE = 256
MESH = pl.DeviceIdType.MESH
CROSS = (2, 5)
SEQUENCE = (0, 1, 3, 2, 4, 5, 6, 7, 8, 9, 10, 11)
PLACES = 6
SPLIT = {10: 2, 11: 2}
EARLY = 4
EARLY_LAGS = (1, 2, 4)
MID_LAGS = (0, 1, 3)
LAST_LAGS = (0, 2, 5)


def bits_of(count):
    bits = count.bit_length() - 1
    assert count == 1 << bits
    return bits


def dot(left, right, left_dim, right_dim):
    return lax.dot_general(
        left, right, (((left_dim,), (right_dim,)), ((), ())), preferred_element_type=jnp.float32
    )


def wide(left, state, state_dim):
    high = state.astype(jnp.bfloat16)
    rest = (state - high.astype(jnp.float32)).astype(jnp.bfloat16)
    return dot(left, high, 1, state_dim) + dot(left, rest, 1, state_dim)


def lanes(start, size):
    return pl.ds(pl.multiple_of(start, COLS), size)


def step_kernel(seq_count, batch_count, grad_scale, names, x_hbm, w_hbm, c_hbm, a_hbm, t_hbm, o_hbm, *scratch):
    m = types.SimpleNamespace(**dict(zip(names, scratch)))
    bits = bits_of(seq_count) - 1
    chips = 1 << bits
    rows, width = x_hbm.shape
    head_width = c_hbm.shape[1]
    groups = head_width // PAIR
    pairs = 3 * groups
    chunks = 2 * pairs
    half = width // 2
    own_rows = width // seq_count
    rank = lax.axis_index("seq")
    core = rank % 2
    chip = rank // 2
    plane = lax.axis_index("batch")
    middle = batch_count // 2
    low_side = plane < middle
    depth = jnp.where(low_side, middle - 1 - plane, plane - middle)
    has_outer = jnp.where(low_side, plane > 0, plane < batch_count - 1)
    is_inner = depth == 0
    inner = jnp.where(low_side, plane + 1, plane - 1)
    outer = jnp.where(low_side, plane - 1, plane + 1)
    mate_id = {"seq": rank ^ 1}

    base = list(range(bits))
    turned = base[bits // 2 :] + base[: bits // 2]
    ways = [base, turned]
    crossed = set(CROSS) if batch_count == 4 else set()
    assert sorted(SEQUENCE) == list(range(pairs))
    places = [(pair, sub) for pair in SEQUENCE for sub in range(SPLIT.get(pair, 1))]

    def units_of(position):
        pair, sub = places[position]
        count = SPLIT.get(pair, 1)
        return [
            types.SimpleNamespace(
                position=position,
                chunk=2 * pair + side,
                side=side,
                sub=sub,
                count=count,
                crossed=pair in crossed,
                place=(position % PLACES) * 2 + side,
                kept=own_rows // 2 if pair in crossed else own_rows // count,
                rows=pl.ds(sub * (own_rows // count), own_rows // count),
                first=sub * (own_rows // count),
            )
            for side in range(2)
        ]

    def earlier(unit):
        if unit.position < PLACES:
            return None
        return units_of(unit.position - PLACES)[unit.side]

    def local(source, target, sem):
        return pltpu.make_async_copy(source, target, sem)

    def remote(source, target, send, recv, device):
        return pltpu.make_async_remote_copy(
            src_ref=source, dst_ref=target, send_sem=send, recv_sem=recv, device_id=device, device_id_type=MESH
        )

    def w_part(group, part):
        column = lanes(part * head_width + group * PAIR, PAIR)
        return local(w_hbm.at[:, column], m.w_parts.at[part], m.w_sem.at[part])

    def w_tile(index):
        row = pl.ds(pl.multiple_of(index * TILE, TILE), TILE)
        return local(w_hbm.at[row], m.w_tiles.at[index % 2], m.t_sem.at[index % 2])

    def t_out(index):
        return local(m.t_tile.at[index % 2], t_hbm.at[:, lanes(index * TILE, TILE)], m.t_sem.at[2 + index % 2])

    def a_out(group):
        column = pl.ds(group * PAIR, PAIR)
        return local(m.grads.at[:, column], a_hbm.at[:, column], m.a_sem.at[group])

    def o_out(unit):
        group, spot = unit.chunk // 6, unit.chunk % 6
        column = (spot % 3) * head_width + group * PAIR + (spot // 3) * COLS
        row = unit.rows
        return local(m.from_inner.at[unit.chunk, row], o_hbm.at[row, pl.ds(column, COLS)], m.o_sem.at[unit.place])

    x_in = local(x_hbm, m.x_all, m.x_sem.at[0])
    c_in = local(c_hbm, m.grads, m.x_sem.at[1])
    for part in range(3):
        w_part(0, part).start()
        if part == 0:
            x_in.start()
    c_in.start()
    barrier = pltpu.get_barrier_semaphore()
    pl.semaphore_signal(barrier, inc=1, device_id=mate_id, device_id_type=MESH)
    for bit in range(bits):
        pl.semaphore_signal(barrier, inc=1, device_id={"seq": rank ^ (2 << bit)}, device_id_type=MESH)
    pl.semaphore_signal(barrier, inc=1, device_id={"batch": inner}, device_id_type=MESH)

    @pl.when(has_outer)
    def _():
        pl.semaphore_signal(barrier, inc=1, device_id={"batch": outer}, device_id_type=MESH)

    position = rank * rows + lax.broadcasted_iota(jnp.int32, (rows, COLS), 0)
    m.scale[...] = DH ** (-0.5) / jnp.sqrt(position.astype(jnp.float32) + 1.0)

    def project(group):
        @pl.loop(0, 3)
        def _(part):
            w_part(group, part).wait()
            m.qkv[:, lanes(part * head_width + group * PAIR, PAIR)] = dot(
                m.x_all[...], m.w_parts[part], 1, 0
            ).astype(m.qkv.dtype)
            if group + 1 < groups:
                w_part(group + 1, part).start()

    def head_columns(group, head):
        start = group * PAIR + head * DH
        return [lanes(part * head_width + start, DH) for part in range(3)] + [lanes(start, DH)]

    def first_swap(group):
        return remote(
            m.states.at[group, 1 - core], m.mates.at[group], m.swap_send.at[0, group], m.swap_recv.at[0, group], mate_id
        )

    def last_swap(group):
        return remote(
            m.gives.at[group], m.carry.at[group, core], m.swap_send.at[1, group], m.swap_recv.at[1, group], mate_id
        )

    def bit_swap(group, bit):
        return remote(
            m.totals.at[bit, group],
            m.others.at[bit, group],
            m.bit_send.at[bit, group],
            m.bit_recv.at[bit, group],
            {"seq": rank ^ (2 << bit)},
        )

    def takes(bit):
        return ((chip // (1 << bit)) % 2) != core

    def make_states(group):
        @pl.loop(0, 2)
        def _(head):
            q_at, k_at, v_at, g_at = head_columns(group, head)
            grad = (m.grads[:, g_at].astype(jnp.float32) * m.scale[...]).astype(jnp.bfloat16)
            m.grads[:, g_at] = grad
            m.states[group, 0, head] = dot(m.qkv[:, k_at], m.qkv[:, v_at], 0, 0)
            m.states[group, 1, head] = dot(m.qkv[:, q_at], grad, 0, 0)

        first_swap(group).start()

    def start_bit(group, bit):
        if bit == bits - 1:
            pl.when(jnp.logical_not(takes(bit)))(bit_swap(group, bit).start)
        else:
            bit_swap(group, bit).start()

    def chain_first(group):
        first_swap(group).wait_recv()
        m.totals[0, group] = m.states[group, core] + m.mates[group]
        start_bit(group, 0)
        m.carry[group, core] = jnp.zeros(m.mates.shape[1:], jnp.float32)

    def chain_bit(group, bit):
        last = bit == bits - 1
        if not last:
            bit_swap(group, bit).wait_recv()
            m.totals[bit + 1, group] = m.totals[bit, group] + m.others[bit, group]
            start_bit(group, bit + 1)

        @pl.when(takes(bit))
        def _():
            if last:
                bit_swap(group, bit).wait_recv()
            m.carry[group, core] += m.others[bit, group]

        if last:
            m.gives[group] = m.carry[group, core] + m.states[group, core]
            last_swap(group).start()

    chains = [
        [functools.partial(chain_first, group)] + [functools.partial(chain_bit, group, bit) for bit in range(bits)]
        for group in range(groups)
    ]

    def chain(group, count=None):
        count = len(chains[group]) if count is None else count
        for _ in range(min(count, len(chains[group]))):
            chains[group].pop(0)()

    def in_block(group, first=0, count=2):
        low = slice(0, TILE)
        high = slice(TILE, BLK)
        row = lax.broadcasted_iota(jnp.int32, (TILE, TILE), 0)
        col = lax.broadcasted_iota(jnp.int32, (TILE, TILE), 1)
        causal = row >= col

        @pl.loop(first, first + count)
        def _(head):
            q_at, k_at, v_at, g_at = head_columns(group, head)
            out_at = lanes(head * DH, DH)

            def products(left_ref, left_at, right_at):
                def one(i, j, masked):
                    value = dot(left_ref[i, left_at], m.qkv[j, right_at], 1, 1)
                    if masked:
                        value = jnp.where(causal, value, 0.0)
                    return value.astype(jnp.bfloat16)

                m.tri[0] = one(low, low, True)
                m.tri[1] = one(high, low, False)
                m.tri[2] = one(high, high, True)

            def by_rows(index, ref, at):
                m.parts[index, low, out_at] = dot(m.tri[0], ref[low, at], 1, 0)
                m.parts[index, high, out_at] = dot(m.tri[1], ref[low, at], 1, 0) + dot(m.tri[2], ref[high, at], 1, 0)

            def by_columns(index, ref, at):
                m.parts[index, low, out_at] = dot(m.tri[0], ref[low, at], 0, 0) + dot(m.tri[1], ref[high, at], 0, 0)
                m.parts[index, high, out_at] = dot(m.tri[2], ref[high, at], 0, 0)

            products(m.qkv, q_at, k_at)
            by_rows(0, m.qkv, v_at)
            by_columns(3, m.grads, g_at)
            products(m.grads, g_at, v_at)
            by_rows(1, m.qkv, k_at)
            by_columns(2, m.qkv, q_at)

    def grad_swap(group, spot):
        slot = group % 2
        return remote(
            m.g_send.at[slot, spot],
            m.g_land.at[slot, spot],
            m.g_ssem.at[slot, spot],
            m.g_rsem.at[slot, spot],
            mate_id,
        )

    def finish(group):
        slot = group % 2
        last_swap(group).wait_recv()

        @pl.loop(0, 2)
        def _(head):
            q_at, k_at, v_at, g_at = head_columns(group, head)
            out_at = lanes(head * DH, DH)
            query, key, value, grad = m.qkv[:, q_at], m.qkv[:, k_at], m.qkv[:, v_at], m.grads[:, g_at]
            kv, gs = m.carry[group, 0, head], m.carry[group, 1, head]

            def give(part, at, result):
                spot = 3 * head + part
                low = result.astype(jnp.bfloat16)
                m.qkv[:, at] = low
                m.g_cat[spot // 2, 0:rows, lanes(spot % 2 * COLS, COLS)] = low
                if group >= 2:
                    grad_swap(group - 2, spot).wait_send()
                m.g_send[slot, spot] = low.astype(jnp.float32)
                grad_swap(group, spot).start()

            give(0, q_at, m.parts[1, :, out_at] + wide(grad, kv, 1))
            give(1, k_at, m.parts[2, :, out_at] + wide(value, gs, 1))
            give(2, v_at, m.parts[3, :, out_at] + wide(key, gs, 0))
            attended = (m.parts[0, :, out_at] + wide(query, kv, 0)) * m.scale[...]
            m.grads[:, g_at] = attended.astype(jnp.bfloat16)

        a_out(group).start()

    spare = rows // COLS

    def x_swap(index):
        row = pl.ds(pl.multiple_of(index * own_rows, own_rows), own_rows)
        return remote(
            m.mine.at[pl.ds(chunks - spare, spare), row],
            m.mine.at[pl.ds(chunks - 2 * spare, spare), row],
            m.x_send.at[index],
            m.x_recv.at[index],
            mate_id,
        )

    def turn_tokens(first, last):
        @pl.loop(first, last)
        def _(index):
            owner = chip ^ index
            m.turned[...] = m.x_all[:, lanes(owner * 2 * own_rows, 2 * own_rows)].T
            row = pl.ds(pl.multiple_of(index * own_rows, own_rows), own_rows)
            m.x_cat[row, 0:rows] = m.turned[pl.ds(pl.multiple_of(core * own_rows, own_rows), own_rows), :]
            other = m.turned[pl.ds(pl.multiple_of((1 - core) * own_rows, own_rows), own_rows), :]
            for piece in range(spare):
                m.mine[chunks - spare + piece, row, :] = other[:, piece * COLS : (piece + 1) * COLS].astype(jnp.float32)
            x_swap(index).start()

    def join_tokens():
        @pl.loop(0, chips)
        def _(index):
            x_swap(index).wait_recv()
            row = pl.ds(pl.multiple_of(index * own_rows, own_rows), own_rows)
            for piece in range(spare):
                at = rows + piece * COLS
                m.x_cat[row, at : at + COLS] = m.mine[chunks - 2 * spare + piece, row, :].astype(jnp.bfloat16)

    keeps_low = jnp.where(is_inner, 0, 1)

    ready = set()

    def multiply(pair):
        group = pair // 3
        ready.add(pair)
        for side in range(2):
            spot = 2 * (pair % 3) + side
            grad_swap(group, spot).wait_recv()
            m.g_cat[spot // 2, rows : 2 * rows, side * COLS : (side + 1) * COLS] = m.g_land[group % 2, spot].astype(
                jnp.bfloat16
            )
        if pair == (chunks - spare) // 2:
            for index in range(chips):
                x_swap(index).wait_send()
        count = 2 if pair in crossed else SPLIT.get(pair, 1)

        @pl.loop(0, chips)
        def _(index):
            value = dot(
                m.x_cat[pl.ds(pl.multiple_of(index * own_rows, own_rows), own_rows), :], m.g_cat[pair % 3], 1, 0
            )
            for side, way in enumerate(ways):
                spot = sum((index // (1 << bit) % 2) * (1 << (bits - 1 - k)) for k, bit in enumerate(way))
                part_rows = own_rows // count
                for sub in range(count):
                    block = sub
                    if pair in crossed:
                        block = 1 - keeps_low if sub == 0 else keeps_low
                    row = pl.multiple_of((block * chips + spot) * part_rows, part_rows)
                    m.mine[2 * pair + side, pl.ds(row, part_rows), :] = value[
                        sub * part_rows : (sub + 1) * part_rows, side * COLS : (side + 1) * COLS
                    ]

        if pair in crossed:
            for unit in units_of(places.index((pair, 0))):
                cross_copy(unit).start()

    def cross_copy(unit):
        index = CROSS.index(unit.chunk // 2) * 2 + unit.side
        return remote(
            m.mine.at[unit.chunk, pl.ds(half // 2, half // 2)],
            m.cross_land.at[index],
            m.cross_send.at[index],
            m.cross_recv.at[index],
            {"batch": plane ^ 1},
        )

    def step_size(unit, step):
        whole = half // 2 if unit.crossed else half // unit.count
        return whole >> (step + 1), unit.sub * whole

    def landing(unit, step):
        size, _ = step_size(unit, step)
        return m.lands[step].at[unit.place, pl.ds(0, size)]

    def step_copy(unit, step):
        size, start = step_size(unit, step)
        return remote(
            m.mine.at[unit.chunk, pl.ds(start + size, size)],
            landing(unit, step),
            m.step_send.at[step, unit.place],
            m.step_recv.at[step, unit.place],
            {"seq": rank ^ (2 << ways[unit.side][step])},
        )

    def start_step(unit, step):
        before = earlier(unit)
        if before is not None:
            step_copy(before, step).wait_send()
        step_copy(unit, step).start()

    lone = batch_count == 2

    def inward_copy(unit, leaf, to_inner):
        _, start = step_size(unit, 0)
        if leaf:
            source = m.mine.at[unit.chunk, pl.ds(start, unit.kept)]
        else:
            source = m.from_outer.at[unit.chunk, unit.rows]
        if to_inner:
            target = m.from_inner.at[unit.chunk, unit.rows]
        else:
            target = m.from_outer.at[unit.chunk, pl.ds(unit.first, unit.kept)]
        return remote(
            source,
            target,
            m.z_send.at[0, unit.place],
            m.z_recv.at[1 if to_inner else 0, unit.place],
            {"batch": inner},
        )

    def outward(unit):
        both = m.from_inner.at[unit.chunk, unit.rows]
        return remote(both, both, m.z_send.at[1, unit.place], m.z_recv.at[1, unit.place], {"batch": outer})

    def start_inward(unit, leaf, to_inner):
        before = earlier(unit)
        if before is not None:
            inward_copy(before, leaf, to_inner).wait_send()
        inward_copy(unit, leaf, to_inner).start()

    def leave(unit):
        @pl.when(jnp.logical_not(has_outer))
        def _():
            start_inward(unit, True, lone)

    def halve(unit, step):
        step_copy(unit, step).wait_recv()
        size, start = step_size(unit, step)
        land = landing(unit, step)
        if step + 1 < bits:
            part = size // 2
            m.mine[unit.chunk, pl.ds(start + part, part), :] += land[pl.ds(part, part), :]
            start_step(unit, step + 1)
            m.mine[unit.chunk, pl.ds(start, part), :] += land[pl.ds(0, part), :]
        else:
            m.mine[unit.chunk, pl.ds(start, size), :] += land[...]
            leave(unit)

    def gather(unit):
        if lone:
            return
        _, start = step_size(unit, 0)
        kept = unit.kept

        @pl.when(has_outer)
        def _():
            inward_copy(unit, True, False).wait_recv()
            if unit.crossed:
                m.from_outer[unit.chunk, pl.ds(kept, kept), :] = m.mine[unit.chunk, pl.ds(start, kept), :]
            else:
                m.from_outer[unit.chunk, pl.ds(unit.first, kept), :] += m.mine[unit.chunk, pl.ds(start, kept), :]

        @pl.when(has_outer & is_inner)
        def _():
            start_inward(unit, False, True)

        if batch_count > 4:

            @pl.when(has_outer & jnp.logical_not(is_inner))
            def _():
                start_inward(unit, False, False)

    def write_out(unit):
        before = earlier(unit)
        if before is not None:
            o_out(before).wait()
        o_out(unit).start()

    def close(unit):
        row = unit.rows
        before = earlier(unit)

        @pl.when(is_inner)
        def _():
            inward_copy(unit, lone, True).wait_recv()
            own = m.mine[unit.chunk, row, :] if lone else m.from_outer[unit.chunk, row, :]
            m.from_inner[unit.chunk, row, :] = (m.from_inner[unit.chunk, row, :] + own) * grad_scale

        @pl.when(is_inner & has_outer)
        def _():
            if before is not None:
                outward(before).wait_send()
            outward(unit).start()

        pl.when(is_inner)(lambda: write_out(unit))

    def take(unit):
        before = earlier(unit)

        @pl.when(jnp.logical_not(is_inner))
        def _():
            inward_copy(unit, lone, True).wait_recv()

        if batch_count > 4:

            @pl.when(jnp.logical_not(is_inner) & has_outer)
            def _():
                if before is not None:
                    outward(before).wait_send()
                outward(unit).start()

        pl.when(jnp.logical_not(is_inner))(lambda: write_out(unit))

    tiles = width // TILE

    def token_tiles(first, count):
        @pl.loop(first, first + count)
        def _(index):
            w_tile(index).wait()

            @pl.when(index >= 2)
            def _():
                t_out(index - 2).wait()

            m.t_tile[index % 2] = dot(m.qkv[...], m.w_tiles[index % 2], 1, 1).astype(m.t_tile.dtype)
            t_out(index).start()

            @pl.when(index + 2 < tiles)
            def _():
                w_tile(index + 2).start()

    def open_place(position):
        assert places[position][0] in ready
        for unit in units_of(position):
            if unit.crossed:
                cross_copy(unit).wait_recv()
                index = CROSS.index(unit.chunk // 2) * 2 + unit.side
                part = half // 4
                upper = pl.ds(part, part)
                m.mine[unit.chunk, upper, :] += m.cross_land[index, upper, :]
                start_step(unit, 0)
                lower = pl.ds(0, part)
                m.mine[unit.chunk, lower, :] += m.cross_land[index, lower, :]
            else:
                start_step(unit, 0)

    events = {}
    for position in range(len(places)):
        for order, unit in enumerate(units_of(position)):
            stages = [functools.partial(halve, unit, step) for step in range(bits)]
            for number, stage in enumerate(stages):
                events.setdefault(position + number, []).append((0, -number, order, stage))
            late = EARLY_LAGS if position < EARLY else (MID_LAGS if unit.count == 1 else LAST_LAGS)
            for number, (stage, lag) in enumerate(zip((gather, close, take), late)):
                events.setdefault(position + bits + lag, []).append(
                    (1, number, order, functools.partial(stage, unit))
                )

    def run_events(slot):
        for _, _, _, event in sorted(events.get(slot, []), key=lambda item: item[:3]):
            event()

    x_in.wait()
    project(0)
    c_in.wait()
    pl.semaphore_wait(barrier, bits + 2 + has_outer.astype(jnp.int32))
    make_states(0)
    turn_tokens(0, 1)
    chain(0, 1)
    turn_tokens(1, chips)
    project(1)
    make_states(1)
    in_block(0, 0, 1)
    chain(0, 1)
    in_block(0, 1, 1)
    chain(1, 1)
    chain(0)
    finish(0)
    join_tokens()
    chain(1, 1)
    multiply(0)
    open_place(0)
    multiply(1)
    open_place(1)
    multiply(2)
    chain(1)
    for index in range(2):
        w_tile(index).start()
    project(2)
    make_states(2)
    project(3)
    run_events(0)
    make_states(3)
    chain(2, 1)
    chain(3, 1)
    ahead = {
        1: [
            lambda: in_block(1),
            lambda: finish(1),
            lambda: multiply(3),
            lambda: open_place(2),
            lambda: multiply(4),
            lambda: multiply(5),
        ],
    }
    opens = {0: [], 1: [3]}
    after = {
        1: [lambda: in_block(2), lambda: chain(2, 1), lambda: chain(3, 1)],
        2: [lambda: chain(2), lambda: chain(3)],
        3: [lambda: finish(2), lambda: in_block(3), lambda: multiply(6)],
        4: [lambda: multiply(7), lambda: multiply(8)],
        5: [lambda: finish(3)],
        6: [lambda: multiply(9), lambda: multiply(10)],
        7: [lambda: multiply(11)],
    }
    for index in range(tiles // 2):
        after.setdefault(8 + index, []).append(functools.partial(token_tiles, 2 * index, 2))
    for slot in range(max(max(events), max(after)) + 1):
        for task in ahead.get(slot, []):
            task()
        if slot:
            run_events(slot)
        for position in opens.get(slot, [slot + 2]):
            if position < len(places):
                open_place(position)
        for task in after.get(slot, []):
            task()

    for index in range(tiles - 2, tiles):
        t_out(index).wait()
    for group in range(groups):
        a_out(group).wait()
        first_swap(group).wait_send()
        last_swap(group).wait_send()
        for bit in range(bits):
            if bit == bits - 1:
                pl.when(jnp.logical_not(takes(bit)))(bit_swap(group, bit).wait_send)
            else:
                bit_swap(group, bit).wait_send()
        if group >= groups - 2:
            for spot in range(6):
                grad_swap(group, spot).wait_send()
    for position in range(len(places)):
        for unit in units_of(position):
            if unit.crossed:
                cross_copy(unit).wait_send()
            if position < len(places) - PLACES:
                continue
            for step in range(bits):
                step_copy(unit, step).wait_send()
            if lone:
                inward_copy(unit, True, True).wait_send()
            else:

                @pl.when(jnp.logical_not(has_outer))
                def _():
                    inward_copy(unit, True, False).wait_send()

                @pl.when(has_outer & is_inner)
                def _():
                    inward_copy(unit, False, True).wait_send()

                if batch_count > 4:

                    @pl.when(has_outer & jnp.logical_not(is_inner))
                    def _():
                        inward_copy(unit, False, False).wait_send()

                @pl.when(has_outer)
                def _():
                    outward(unit).wait_send()

            o_out(unit).wait()


def body(tokens, w_qkv, cotangent):
    rows, width = tokens.shape[1:]
    columns = w_qkv.shape[1]
    head_width = columns // 3
    assert rows == BLK and head_width == HEADS * DH
    seq_count = lax.axis_size("seq")
    batch_count = lax.axis_size("batch")
    bits = bits_of(seq_count) - 1
    groups = head_width // PAIR
    chunks = columns // COLS
    half = width // 2
    own_rows = width // seq_count
    crossed = max(2 * len(CROSS), 1)
    places = 2 * PLACES
    grad_scale = float(batch_count * seq_count * rows) ** -0.5
    f32, bf16 = jnp.float32, jnp.bfloat16
    state = (2, DH, DH)
    sizes = dict(
        x_all=pltpu.VMEM((rows, width), bf16),
        x_cat=pltpu.VMEM((half, 2 * rows), bf16),
        turned=pltpu.VMEM((2 * own_rows, rows), bf16),
        w_parts=pltpu.VMEM((3, width, PAIR), bf16),
        w_tiles=pltpu.VMEM((2, TILE, columns), bf16),
        t_tile=pltpu.VMEM((2, rows, TILE), bf16),
        qkv=pltpu.VMEM((rows, columns), bf16),
        grads=pltpu.VMEM((rows, head_width), bf16),
        scale=pltpu.VMEM((rows, COLS), f32),
        parts=pltpu.VMEM((4, rows, PAIR), f32),
        tri=pltpu.VMEM((3, TILE, TILE), bf16),
        states=pltpu.VMEM((groups, 2) + state, f32),
        mates=pltpu.VMEM((groups,) + state, f32),
        gives=pltpu.VMEM((groups,) + state, f32),
        totals=pltpu.VMEM((bits, groups) + state, f32),
        others=pltpu.VMEM((bits, groups) + state, f32),
        carry=pltpu.VMEM((groups, 2) + state, f32),
        g_send=pltpu.VMEM((2, 6, rows, COLS), f32),
        g_land=pltpu.VMEM((2, 6, rows, COLS), f32),
        g_cat=pltpu.VMEM((3, 2 * rows, PAIR), bf16),
        mine=pltpu.VMEM((chunks, half, COLS), f32),
        lands=[pltpu.VMEM((places, half >> (step + 1), COLS), f32) for step in range(bits)],
        cross_land=pltpu.VMEM((crossed, half // 2, COLS), f32),
        from_outer=pltpu.VMEM((chunks, own_rows, COLS), f32),
        from_inner=pltpu.VMEM((chunks, own_rows, COLS), f32),
        w_sem=pltpu.SemaphoreType.DMA((3,)),
        x_sem=pltpu.SemaphoreType.DMA((2,)),
        x_send=pltpu.SemaphoreType.DMA((1 << bits,)),
        x_recv=pltpu.SemaphoreType.DMA((1 << bits,)),
        t_sem=pltpu.SemaphoreType.DMA((4,)),
        a_sem=pltpu.SemaphoreType.DMA((groups,)),
        o_sem=pltpu.SemaphoreType.DMA((places,)),
        swap_send=pltpu.SemaphoreType.DMA((2, groups)),
        swap_recv=pltpu.SemaphoreType.DMA((2, groups)),
        bit_send=pltpu.SemaphoreType.DMA((bits, groups)),
        bit_recv=pltpu.SemaphoreType.DMA((bits, groups)),
        g_ssem=pltpu.SemaphoreType.DMA((2, 6)),
        g_rsem=pltpu.SemaphoreType.DMA((2, 6)),
        cross_send=pltpu.SemaphoreType.DMA((crossed,)),
        cross_recv=pltpu.SemaphoreType.DMA((crossed,)),
        step_send=pltpu.SemaphoreType.DMA((bits, places)),
        step_recv=pltpu.SemaphoreType.DMA((bits, places)),
        z_send=pltpu.SemaphoreType.DMA((2, places)),
        z_recv=pltpu.SemaphoreType.DMA((2, places)),
    )
    attended, token_grad, weight_grad = pl.pallas_call(
        functools.partial(step_kernel, seq_count, batch_count, grad_scale, tuple(sizes)),
        out_shape=(
            jax.ShapeDtypeStruct((rows, head_width), bf16),
            jax.ShapeDtypeStruct((rows, width), bf16),
            jax.ShapeDtypeStruct((own_rows, columns), f32),
        ),
        in_specs=[pl.BlockSpec(memory_space=pl.ANY)] * 3,
        out_specs=[pl.BlockSpec(memory_space=pl.ANY)] * 3,
        scratch_shapes=list(sizes.values()),
        compiler_params=pltpu.CompilerParams(
            collective_id=0, has_side_effects=True, vmem_limit_bytes=60 * 1024 * 1024
        ),
    )(tokens[0], w_qkv, cotangent[0])
    return attended[None], token_grad[None], weight_grad


def solution(mesh):
    return jax.shard_map(
        body,
        mesh=mesh,
        in_specs=(P("batch", "seq", None), P(), P("batch", "seq", None)),
        out_specs=(P("batch", "seq", None), P("batch", "seq", None), P("seq", None)),
        check_vma=False,
    )
```
